32 devices in a mesh: chain: 4 (over z), ctx: 4 (over y, x), tp: 2 (over core).
Axes of the slice: x: 2, y: 2, z: 4, core: 2. Of those that a mesh axis runs over, the one named last changes fastest.
Arguments:
- tokens: bfloat16 [16384, 2048], P(('chain', 'ctx')), may hold values from -6 to 6
- w_in: bfloat16 [2048, 3, 2, 1024], P(None, None, 'tp'), may hold values from -0.125 to 0.125
- conv_w: float32 [3, 3, 2, 1024], P(None, None, 'tp'), may hold values from -3 to 3
- w_q: bfloat16 [2048, 256], replicated, may hold values from -0.125 to 0.125
- w_k: bfloat16 [2048, 256], replicated, may hold values from -0.125 to 0.125
- gain: float32 [2, 1024], P('tp'), may hold values from 0.1 to 1.9
- w_o: bfloat16 [2, 1024, 2048], P('tp'), may hold values from -0.125 to 0.125
Outputs:
- out: bfloat16 [16384, 2048], P(('chain', 'ctx', 'tp'))
The draws below stay inside these ranges and needn't reach their ends.
All inputs are finite; a program needn't handle non-finite values.
Results may differ from the reference program's by a relative error of at most 0.013.
Values may be sent and summed in bfloat16 or wider, within the bound.
No kernel may reach another device: no remote copies, remote signals or barrier semaphores. Data moves between devices by JAX's collectives and lax.ppermute only.
A program may use at most 192 MiB of HBM per device.

```python
import math
import jax
import jax.numpy as jnp
from jax import lax

D = 2048
H = 16
HD = 128
F = 16
TAPS = 3
HALF = 1024
SEQ = 16384


def levels(own_key, shape, cuts, low, top_value):
    level, own = 1.0, jax.random.fold_in(own_key, 6)
    for position, blocks in cuts:
        draws = jnp.exp(jax.random.uniform(jax.random.fold_in(own, position), (blocks,), jnp.float32, low / len(cuts), top_value / len(cuts)))
        level = level * jnp.repeat(draws, shape[position] // blocks).reshape([-1 if axis == position else 1 for axis in range(len(shape))])
    return level


def noise(own_key, extent, width, reach, shards=(), kind=jnp.bfloat16):
    drawn = width * jax.random.normal(own_key, extent, jnp.float32)
    if shards:
        drawn = drawn * levels(own_key, extent, shards, -0.22, 0.18)
    return jnp.clip(drawn, -reach, reach).astype(kind)


def setup_inputs(seed: int = 0) -> dict:
    seeds = jax.random.split(jax.random.key(seed), 8)
    return {
        "tokens": noise(seeds[0], (SEQ, D), 1.0, 6.0, ((0, 16),)),
        "w_in": noise(seeds[1], (D, 3, 2, HALF), D ** -0.5, 0.125, ((2, 2),)),
        "conv_w": noise(seeds[2], (TAPS, 3, 2, HALF), 0.6, 3.0, ((2, 2),), jnp.float32),
        "w_q": noise(seeds[3], (D, H * F), D ** -0.5, 0.125),
        "w_k": noise(seeds[4], (D, H * F), D ** -0.5, 0.125),
        "gain": jnp.clip(1.0 + 0.18 * jax.random.normal(seeds[5], (2, HALF), jnp.float32), 0.1, 1.9),
        "w_o": noise(seeds[6], (2, HALF, D), (2 * HALF) ** -0.5, 0.125, ((0, 2),)),
    }


EPS = 1e-05
HIGH = lax.Precision.HIGHEST

def second_order(inputs):
    widened = inputs.astype(jnp.float32)
    feature = inputs.shape[-1]
    products = widened[..., :, None] * widened[..., None, :] * (1.0 / math.sqrt(2.0 * feature))
    return products.reshape(inputs.shape[:-1] + (feature * feature,)).astype(jnp.bfloat16)

def reference(tokens, w_in, conv_w, w_q, w_k, gain, w_o):
    seq_len = tokens.shape[0]
    half_width = w_in.shape[3]
    head_half = HD // 2
    projected = jnp.dot(tokens, w_in.reshape(D, 6 * half_width), preferred_element_type=jnp.float32).astype(jnp.bfloat16)
    projected = projected.reshape(seq_len, 3, 2, half_width)
    lag_one = jnp.concatenate([jnp.zeros((1, 3, 2, half_width), jnp.bfloat16), projected[:-1]], axis=0)
    lag_two = jnp.concatenate([jnp.zeros((2, 3, 2, half_width), jnp.bfloat16), projected[:-2]], axis=0)
    convolved = (conv_w[0] * projected.astype(jnp.float32) + conv_w[1] * lag_one.astype(jnp.float32) + conv_w[2] * lag_two.astype(jnp.float32)).astype(jnp.bfloat16)
    values = convolved[:, 0].reshape(seq_len, 2, H, head_half).transpose(0, 2, 1, 3).reshape(seq_len, H, HD)
    queries = jnp.dot(tokens, w_q, preferred_element_type=jnp.float32).astype(jnp.bfloat16).reshape(seq_len, H, F)
    keys = jnp.dot(tokens, w_k, preferred_element_type=jnp.float32).astype(jnp.bfloat16).reshape(seq_len, H, F)
    block_len = min(512, seq_len)
    block_count = seq_len // block_len
    inv_root = 1.0 / math.sqrt(F)
    causal = lax.broadcasted_iota(jnp.int32, (block_len, block_len), 0) >= lax.broadcasted_iota(jnp.int32, (block_len, block_len), 1)

    def advance(carry, pieces):
        quad_state, line_state, flat_state = carry
        query_part, key_part, value_part = pieces
        query_wide = second_order(query_part).astype(jnp.float32)
        key_wide = second_order(key_part).astype(jnp.float32)
        query_flt = query_part.astype(jnp.float32)
        key_flt = key_part.astype(jnp.float32)
        value_flt = value_part.astype(jnp.float32)
        carried = jnp.einsum('bhf,hfe->bhe', query_wide, quad_state, precision=HIGH) + jnp.einsum('bhf,hfe->bhe', query_flt, line_state, precision=HIGH) * inv_root + flat_state[None]
        kernel = 1.0 + jnp.einsum('bhf,chf->hbc', query_flt, key_flt, precision=HIGH) * inv_root + jnp.einsum('bhf,chf->hbc', query_wide, key_wide, precision=HIGH)
        kernel = jnp.where(causal[None], kernel, 0.0).astype(jnp.bfloat16).astype(jnp.float32)
        inside = jnp.einsum('hbc,che->bhe', kernel, value_flt, precision=HIGH)
        quad_state = quad_state + jnp.einsum('bhf,bhe->hfe', key_wide, value_flt, precision=HIGH)
        line_state = line_state + jnp.einsum('bhf,bhe->hfe', key_flt, value_flt, precision=HIGH)
        flat_state = flat_state + lax.optimization_barrier(jnp.sum(value_flt, axis=0))
        return ((quad_state, line_state, flat_state), carried + inside)
    start = (jnp.zeros((H, F * F, HD), jnp.float32), jnp.zeros((H, F, HD), jnp.float32), jnp.zeros((H, HD), jnp.float32))
    pieces = (queries.reshape(block_count, block_len, H, F), keys.reshape(block_count, block_len, H, F), values.reshape(block_count, block_len, H, HD))
    final_state, attended = lax.scan(advance, start, pieces)
    attended = attended.reshape(seq_len, H, 2, head_half)
    mean_sq = lax.optimization_barrier(jnp.mean(attended * attended, axis=-1, keepdims=True))
    normed = (attended * lax.rsqrt(mean_sq + EPS)).astype(jnp.bfloat16)
    normed = normed.transpose(0, 2, 1, 3).reshape(seq_len, 2, half_width)
    mixed = (jax.nn.silu(convolved[:, 1].astype(jnp.float32)) * (normed.astype(jnp.float32) * gain + convolved[:, 2].astype(jnp.float32))).astype(jnp.bfloat16)
    part_zero = jnp.dot(mixed[:, 0], w_o[0], preferred_element_type=jnp.float32).astype(jnp.bfloat16)
    part_one = jnp.dot(mixed[:, 1], w_o[1], preferred_element_type=jnp.float32).astype(jnp.bfloat16)
    part_zero, part_one = lax.optimization_barrier((part_zero, part_one))
    return (part_zero.astype(jnp.float32) + part_one.astype(jnp.float32)).astype(jnp.bfloat16)
```

```python
import functools

import jax
import jax.numpy as jnp
from jax import lax
from jax.experimental import pallas as pl
from jax.experimental.pallas import tpu as pltpu
from jax.sharding import PartitionSpec as P

H = 16
F = 16
EPS = 1e-05
CHUNK = 256
GROUPS = 4
PER = H // GROUPS
SLABS = 10
ROWS = SLABS * F
WIDE = SLABS * PER * F
F32 = jnp.float32
BF16 = jnp.bfloat16
MIB = 1 << 20


def params(mib):
    return pltpu.CompilerParams(vmem_limit_bytes=mib * MIB, dimension_semantics=("arbitrary",))


def dot(a, b):
    return jnp.dot(a, b, preferred_element_type=F32)


def lanes(shape):
    return lax.broadcasted_iota(jnp.int32, shape, len(shape) - 1)


def qk_body(x, wq, wk, q_out, kt_out):
    q_out[...] = dot(x[...], wq[...]).astype(BF16)
    keys = dot(x[...], wk[...]).astype(BF16).astype(F32)
    kt_out[...] = keys.T.astype(BF16)


def project_qk(tokens, w_q, w_k):
    rows, width = tokens.shape
    feats = w_q.shape[1]
    return pl.pallas_call(
        qk_body,
        grid=(rows // CHUNK,),
        in_specs=[
            pl.BlockSpec((CHUNK, width), lambda c: (c, 0)),
            pl.BlockSpec((width, feats), lambda c: (0, 0)),
            pl.BlockSpec((width, feats), lambda c: (0, 0)),
        ],
        out_specs=[
            pl.BlockSpec((CHUNK, feats), lambda c: (c, 0)),
            pl.BlockSpec((feats, CHUNK), lambda c: (0, c)),
        ],
        out_shape=[
            jax.ShapeDtypeStruct((rows, feats), BF16),
            jax.ShapeDtypeStruct((feats, rows), BF16),
        ],
        compiler_params=params(24),
        name="project_qk",
    )(tokens, w_q, w_k)


def convolve(c, halo, x, w, taps, stream, hold):
    @pl.when(c == 0)
    def _():
        hold[0:8] = dot(halo[...], w).astype(BF16).astype(F32)

    @pl.when(c > 0)
    def _():
        hold[0:8] = hold[CHUNK : CHUNK + 8]

    hold[8 : CHUNK + 8] = dot(x[...], w).astype(BF16).astype(F32)
    return (
        taps[0, stream] * hold[8 : CHUNK + 8]
        + taps[1, stream] * hold[7 : CHUNK + 7]
        + taps[2, stream] * hold[6 : CHUNK + 6]
    ).astype(BF16)


def key_features(kt, dup, g):
    own = kt[g * 64 : (g + 1) * 64].astype(F32).reshape(PER, F, CHUNK)
    slabs = []
    for r in range(8):
        slabs.append((own * dup[g * PER : (g + 1) * PER, r : r + F]).astype(BF16))
    row = lax.broadcasted_iota(jnp.int32, own.shape, 1)
    last = jnp.where(row < 8, own * dup[g * PER : (g + 1) * PER, 8 : 8 + F], 0.0)
    slabs.append(jnp.where(row == 8, 1.0, last).astype(BF16))
    slabs.append(own.astype(BF16))
    return jnp.concatenate([s.reshape(PER * F, CHUNK) for s in slabs], axis=0)


def values_body(place, halo, x, w, taps, kt, v_out, before_out, *rest):
    pieces = rest[:-4]
    hold, dup, acc, flat = rest[-4:]
    c = pl.program_id(0)
    values = convolve(c, halo, x, w[0], taps, 0, hold)
    v_out[...] = values

    @pl.when(c == 0)
    def _():
        acc[...] = jnp.zeros_like(acc)

    before_out[0] = acc[...].astype(BF16)
    whole = kt[...].astype(F32).reshape(H, F, CHUNK)
    dup[:, 0:F] = whole
    dup[:, F : 2 * F] = whole
    low = lanes((SLABS, F, 128)) < 64
    for g in range(GROUPS):
        state = dot(key_features(kt, dup, g), values[:, g * 256 : (g + 1) * 256])
        state = state.reshape(SLABS, PER, F, 256)
        left = jnp.where(low, state[:, 0, :, :128], state[:, 1, :, :128])
        right = jnp.where(low, state[:, 2, :, 128:], state[:, 3, :, 128:])
        acc[g, :, :128] += left.reshape(ROWS, 128)
        acc[g, :, 128:] += right.reshape(ROWS, 128)

    @pl.when(c == pl.num_programs(0) - 1)
    def _():
        n = len(pieces)
        flat[...] = acc[...].reshape(n, GROUPS * ROWS // n, 256).astype(BF16)
        for m, piece in enumerate(pieces):
            piece[...] = flat[lax.rem(place[0] + m, n)]


def project_values(place, halo, tokens, w, taps, kt, n):
    rows, width = tokens.shape
    half = w.shape[2]
    part = GROUPS * ROWS // n
    return pl.pallas_call(
        values_body,
        grid_spec=pltpu.PrefetchScalarGridSpec(
            num_scalar_prefetch=1,
            grid=(rows // CHUNK,),
            in_specs=[
                pl.BlockSpec((8, width), lambda c, s: (0, 0)),
                pl.BlockSpec((CHUNK, width), lambda c, s: (c, 0)),
                pl.BlockSpec((1, width, half), lambda c, s: (0, 0, 0)),
                pl.BlockSpec((3, 3, half), lambda c, s: (0, 0, 0)),
                pl.BlockSpec((H * F, CHUNK), lambda c, s: (0, c)),
            ],
            out_specs=[
                pl.BlockSpec((CHUNK, half), lambda c, s: (c, 0)),
                pl.BlockSpec((1, GROUPS, ROWS, 256), lambda c, s: (c, 0, 0, 0)),
            ]
            + [pl.BlockSpec((part, 256), lambda c, s: (0, 0)) for _ in range(n)],
            scratch_shapes=[
                pltpu.VMEM((CHUNK + 8, half), F32),
                pltpu.VMEM((H, 2 * F, CHUNK), F32),
                pltpu.VMEM((GROUPS, ROWS, 256), F32),
                pltpu.VMEM((n, part, 256), BF16),
            ],
        ),
        out_shape=[
            jax.ShapeDtypeStruct((rows, half), BF16),
            jax.ShapeDtypeStruct((rows // CHUNK, GROUPS, ROWS, 256), BF16),
        ]
        + [jax.ShapeDtypeStruct((part, 256), BF16) for _ in range(n)],
        compiler_params=params(40),
        name="project_values",
    )(place, halo, tokens, w, taps, kt)


def stream_body(stream, halo, x, w, taps, out, hold):
    out[...] = convolve(pl.program_id(0), halo, x, w[0], taps, stream, hold)


def project_stream(stream, halo, tokens, w, taps):
    rows, width = tokens.shape
    half = w.shape[2]
    return pl.pallas_call(
        functools.partial(stream_body, stream),
        grid=(rows // CHUNK,),
        in_specs=[
            pl.BlockSpec((8, width), lambda c: (0, 0)),
            pl.BlockSpec((CHUNK, width), lambda c: (c, 0)),
            pl.BlockSpec((1, width, half), lambda c: (stream, 0, 0)),
            pl.BlockSpec((3, 3, half), lambda c: (0, 0, 0)),
        ],
        out_specs=pl.BlockSpec((CHUNK, half), lambda c: (c, 0)),
        out_shape=jax.ShapeDtypeStruct((rows, half), BF16),
        scratch_shapes=[pltpu.VMEM((CHUNK + 8, half), F32)],
        compiler_params=params(32),
        name="project_gate" if stream == 1 else "project_skip",
    )(halo, tokens, w, taps)


def inside_body(place, q, kt, v, out):
    low = lanes((CHUNK, 128)) < 64
    head = lanes((CHUNK, 128)) // F
    causal = lax.broadcasted_iota(jnp.int32, (CHUNK, CHUNK), 0) >= lanes((CHUNK, CHUNK))
    for part in range(2):
        query = q[:, part * 128 : (part + 1) * 128] * 0.25
        stacked = jnp.concatenate(
            [jnp.where(head == h, query, 0.0).astype(BF16) for h in range(8)], axis=0
        )
        score = dot(stacked, kt[part * 128 : (part + 1) * 128])
        for pair in range(4):
            both = []
            at = part * 512 + pair * 128
            for h in (2 * pair, 2 * pair + 1):
                x = score[h * CHUNK : (h + 1) * CHUNK]
                poly = x * (0.5 * x + 1.0) + 1.0
                weight = jnp.where(causal, poly, 0.0).astype(BF16)
                both.append(dot(weight, v[:, at : at + 128]))
            out[:, at : at + 128] = jnp.where(low, both[0], both[1])


def inside(place, q, kt, v, count, start):
    half = v.shape[1]
    return pl.pallas_call(
        inside_body,
        grid_spec=pltpu.PrefetchScalarGridSpec(
            num_scalar_prefetch=1,
            grid=(count,),
            in_specs=[
                pl.BlockSpec((CHUNK, H * F), lambda c, s: (s[start] + c, 0)),
                pl.BlockSpec((H * F, CHUNK), lambda c, s: (0, s[start] + c)),
                pl.BlockSpec((CHUNK, half), lambda c, s: (s[start] + c, 0)),
            ],
            out_specs=pl.BlockSpec((CHUNK, half), lambda c, s: (c, 0)),
        ),
        out_shape=jax.ShapeDtypeStruct((count * CHUNK, half), F32),
        compiler_params=params(24),
        name="inside",
    )(place, q, kt, v)


def spread():
    src = lax.broadcasted_iota(jnp.int32, (H * F, GROUPS * WIDE), 0)
    col = lax.broadcasted_iota(jnp.int32, (H * F, GROUPS * WIDE), 1)
    g, rest = col // WIDE, col % WIDE
    slab, h, i = rest // 64, (rest // F) % PER, rest % F
    shift = jnp.where(slab == 9, 0, slab)
    want = g * 64 + h * F + (i + shift) % F
    scale = jnp.where(slab == 0, 1.0 / 32, jnp.where(slab == 9, 0.25, 1.0 / 16))
    scale = jnp.where((slab == 8) & (i >= 8), 0.0, scale)
    second = jnp.where(src == want, scale, 0.0).astype(BF16)
    src = lax.broadcasted_iota(jnp.int32, (H * F, GROUPS * 128), 0)
    col = lax.broadcasted_iota(jnp.int32, (H * F, GROUPS * 128), 1)
    first = jnp.where(src == (col // 128) * 64 + col % 64, 1.0, 0.0).astype(BF16)
    return first, second


def finish_body(place, q, att, before, gate, skip, gain, w_o, first, second, *rest):
    pieces, (out, start, mixed) = rest[:-3], rest[-3:]
    n = len(pieces)

    @pl.when(pl.program_id(0) == 0)
    def _():
        for m, piece in enumerate(pieces):
            start[lax.rem(place[0] + n - m, n)] = piece[...]

    prefix = start[...].reshape(GROUPS, ROWS, 256).astype(F32)
    lane = lanes((CHUNK, 128))
    one = jnp.where((lane < 64) & (lane % F == 8), 1.0, 0.0)
    wide = lanes((SLABS, F, 256)) // 64
    mean = (lax.broadcasted_iota(jnp.int32, (256, 256), 0) // 64 == lanes((256, 256)) // 64)
    mean = jnp.where(mean, 1.0 / 64, 0.0).astype(BF16)
    lead = dot(q[...], first[...])
    for g in range(GROUPS):
        b = dot(q[...], second[:, g * WIDE : (g + 1) * WIDE])
        a = lead[:, g * 128 : (g + 1) * 128]
        feats = [(a * b[:, s * 128 : (s + 1) * 128]).astype(BF16) for s in range(4)]
        b4 = b[:, 512:640]
        feats.append((jnp.where(lane < 64, a * b4, b4) + one).astype(BF16))
        state = (prefix[g] + before[0, g].astype(F32)).astype(BF16).reshape(SLABS, F, 256)
        state = jnp.stack([jnp.where(wide == h, state, 0.0).astype(BF16) for h in range(PER)], axis=1)
        state = state.reshape(WIDE, 256)
        at = slice(g * 256, (g + 1) * 256)
        whole = att[:, at] + dot(jnp.concatenate(feats, axis=1), state)
        mean_sq = dot((whole * whole).astype(BF16), mean)
        normed = (whole * lax.rsqrt(mean_sq + EPS)).astype(BF16).astype(F32)
        gates = gate[:, at].astype(F32)
        act = gates / (1.0 + jnp.exp(-gates))
        mixed[:, at] = (act * (normed * gain[:, at] + skip[:, at].astype(F32))).astype(BF16)
    out[...] = dot(mixed[...], w_o[...]).astype(BF16)


def finish(place, q, att, before, gate, skip, gain, w_o, first, second, pieces, count, start):
    half, width = w_o.shape
    n = len(pieces)
    part = GROUPS * ROWS // n
    return pl.pallas_call(
        finish_body,
        grid_spec=pltpu.PrefetchScalarGridSpec(
            num_scalar_prefetch=1,
            grid=(count,),
            in_specs=[
                pl.BlockSpec((CHUNK, H * F), lambda c, s: (s[start] + c, 0)),
                pl.BlockSpec((CHUNK, half), lambda c, s: (s[start] + c, 0)),
                pl.BlockSpec((1, GROUPS, ROWS, 256), lambda c, s: (s[start] + c, 0, 0, 0)),
                pl.BlockSpec((CHUNK, half), lambda c, s: (s[start] + c, 0)),
                pl.BlockSpec((CHUNK, half), lambda c, s: (s[start] + c, 0)),
                pl.BlockSpec((1, half), lambda c, s: (0, 0)),
                pl.BlockSpec((half, width), lambda c, s: (0, 0)),
                pl.BlockSpec((H * F, GROUPS * 128), lambda c, s: (0, 0)),
                pl.BlockSpec((H * F, GROUPS * WIDE), lambda c, s: (0, 0)),
            ]
            + [pl.BlockSpec((part, 256), lambda c, s: (0, 0)) for _ in range(n)],
            out_specs=pl.BlockSpec((CHUNK, width), lambda c, s: (c, 0)),
            scratch_shapes=[
                pltpu.VMEM((n, part, 256), BF16),
                pltpu.VMEM((CHUNK, half), BF16),
            ],
        ),
        out_shape=jax.ShapeDtypeStruct((count * CHUNK, width), BF16),
        compiler_params=params(40),
        name="finish",
    )(place, q, att, before, gate, skip, gain, w_o, first, second, *pieces)


def shift(block, axes, distance, size):
    return lax.ppermute(block, axes, [(i, i + distance) for i in range(size - distance)])


def turn(block, axis, distance, size):
    return lax.ppermute(block, axis, [(i, (i + distance) % size) for i in range(size)])


def per_device(tokens, w_in, conv_w, w_q, w_k, gain, w_o):
    rows, width = tokens.shape
    half = w_in.shape[3]
    n, blocks = lax.axis_size("ctx"), lax.axis_size("chain")
    me, core = lax.axis_index("ctx"), lax.axis_index("tp")
    chunks = rows // CHUNK
    per_half = chunks // 2
    place = jnp.stack([me, (1 - core) * per_half, core * per_half, 0 * me]).astype(jnp.int32)
    streams = w_in.transpose(1, 2, 0, 3).reshape(3, width, half)
    taps = conv_w.reshape(3, 3, half)
    weight = w_o.reshape(half, width)

    halo = shift(tokens[rows - 8 :], ("chain", "ctx"), 1, n * blocks)
    q, kt = project_qk(tokens, w_q, w_k)
    values, before, *mine = project_values(place, halo, tokens, streams, taps, kt, n)
    theirs = [mine[0]] + [turn(mine[m], "ctx", m, n) for m in range(1, n)]
    gate = project_stream(1, halo, tokens, streams, taps)
    wide = [t.astype(F32) for t in theirs]
    total = sum(wide).astype(BF16)
    earlier = [shift(total, "chain", d, blocks) for d in range(1, blocks)]
    skip = project_stream(2, halo, tokens, streams, taps)
    base = sum(e.astype(F32) for e in earlier)
    starts = []
    for m in range(n):
        peer = (me + m) % n
        found = base
        for k, part in enumerate(wide):
            found = found + jnp.where((me - k) % n < peer, part, 0.0)
        starts.append(found.astype(BF16))
    got = [starts[0]] + [turn(starts[m], "ctx", m, n) for m in range(1, n)]
    att = inside(place, q, kt, values, chunks, 3)
    first, second = spread()
    tail = (q, att, before, gate, skip, gain, weight, first, second, got, per_half)
    away = finish(place, *tail, 1)
    swapped = lax.ppermute(away, "tp", [(0, 1), (1, 0)])
    home = finish(place, *tail, 2)
    return (home.astype(F32) + swapped.astype(F32)).astype(BF16)


def solution(mesh):
    return jax.shard_map(
        per_device,
        mesh=mesh,
        in_specs=(
            P(("chain", "ctx"), None),
            P(None, None, "tp", None),
            P(None, None, "tp", None),
            P(),
            P(),
            P("tp", None),
            P("tp", None, None),
        ),
        out_specs=P(("chain", "ctx", "tp"), None),
        check_vma=False,
    )
```

```python
import functools

import jax
import jax.numpy as jnp
from jax import lax
from jax.experimental import pallas as pl
from jax.experimental.pallas import tpu as pltpu
from jax.sharding import PartitionSpec as P

H = 16
F = 16
EPS = 1e-05
CHUNK = 256
GROUPS = 4
PER = H // GROUPS
SLABS = 10
ROWS = SLABS * F
WIDE = SLABS * PER * F
F32 = jnp.float32
BF16 = jnp.bfloat16
MIB = 1 << 20


VM = pl.BlockSpec(memory_space=pltpu.VMEM)
ANY = pl.BlockSpec(memory_space=pl.ANY)
SM = pl.BlockSpec(memory_space=pltpu.SMEM)


def params(mib):
    return pltpu.CompilerParams(vmem_limit_bytes=mib * MIB)


def in_hbm(x):
    return pltpu.with_memory_space_constraint(x, pltpu.HBM)


def columns(src, dst, sems, first, count, at=0):
    return [
        pltpu.make_async_copy(
            src.at[:, (first + j) * 256 : (first + j + 1) * 256],
            dst.at[:, (at + j) * 256 : (at + j + 1) * 256],
            sems.at[j],
        )
        for j in range(count)
    ]


def row_copies(src, dst, sems, count):
    size = dst.shape[0] // count
    return [
        pltpu.make_async_copy(
            src.at[i * size : (i + 1) * size], dst.at[i * size : (i + 1) * size], sems.at[i]
        )
        for i in range(count)
    ]


def dot(a, b):
    return jnp.dot(a, b, preferred_element_type=F32)


def lanes(shape):
    return lax.broadcasted_iota(jnp.int32, shape, len(shape) - 1)


def qk_body(x, wq, wk, streams, q_out, kt_out, x_out, w_out, wqk, sems):
    feats = wq.shape[1]
    w_copies = [
        pltpu.make_async_copy(wq, wqk.at[:, 0:feats], sems.at[0]),
        pltpu.make_async_copy(wk, wqk.at[:, feats : 2 * feats], sems.at[1]),
    ]
    x_copies = row_copies(x, x_out, sems.at[2:6], 4)
    later = columns(streams.at[0], w_out, sems.at[6:8], 0, 2)
    for copy in w_copies + x_copies + later:
        copy.start()
    for copy in w_copies:
        copy.wait()
    size = x.shape[0] // 4
    for i, copy in enumerate(x_copies):
        copy.wait()
        at = slice(i * size, (i + 1) * size)
        both = dot(x_out[at], wqk[...]).astype(BF16)
        q_out[at] = both[:, :feats]
        kt_out[:, at] = both[:, feats:].astype(F32).T.astype(BF16)
    for copy in later:
        copy.wait()


def project_qk(tokens, w_q, w_k, streams):
    rows, width = tokens.shape
    feats = w_q.shape[1]
    return pl.pallas_call(
        qk_body,
        in_specs=[ANY] * 4,
        out_specs=[VM] * 4,
        out_shape=[
            pltpu.VMEM((rows, feats), BF16),
            pltpu.VMEM((feats, rows), BF16),
            pltpu.VMEM((rows, width), BF16),
            pltpu.VMEM((width, 512), BF16),
        ],
        scratch_shapes=[pltpu.VMEM((width, 2 * feats), BF16), pltpu.SemaphoreType.DMA((8,))],
        compiler_params=params(16),
        name="project_qk",
    )(in_hbm(tokens), in_hbm(w_q), in_hbm(w_k), streams)


def convolve(halo, x, w, taps, stream, j, hold, out):
    rows = x.shape[0]
    at = slice(j * 256, (j + 1) * 256)
    hold[0:8] = dot(halo[...], w).astype(BF16).astype(F32)
    for a in range(0, rows, 256):
        hold[8 + a : 264 + a] = dot(x[a : a + 256], w).astype(BF16).astype(F32)
    for a in range(0, rows, 256):
        out[a : a + 256, at] = (
            taps[0, stream : stream + 1, at] * hold[8 + a : 264 + a]
            + taps[1, stream : stream + 1, at] * hold[7 + a : 263 + a]
            + taps[2, stream : stream + 1, at] * hold[6 + a : 262 + a]
        ).astype(BF16)


def key_features(kt, dup, g):
    size = kt.shape[1]
    heads = slice(g * PER, (g + 1) * PER)
    own = dup[heads, 0:F]
    slabs = [(own * dup[heads, r : r + F]).astype(BF16) for r in range(8)]
    row = lax.broadcasted_iota(jnp.int32, own.shape, 1)
    last = jnp.where(row < 8, own * dup[heads, 8 : 8 + F], 0.0)
    slabs.append(jnp.where(row == 8, 1.0, last).astype(BF16))
    slabs.append(kt[g * 64 : (g + 1) * 64].reshape(PER, F, size))
    return jnp.concatenate([s.reshape(PER * F, size) for s in slabs], axis=0)


def values_body(place, halo, x, w_early, streams, taps, kt, v_out, before, w_next, *rest):
    pieces, (hold, dup, flat, w_late, sems) = rest[:-5], rest[-5:]
    n = len(pieces)
    rows = x.shape[0]
    late = columns(streams.at[0], w_late, sems.at[0:2], 2, 2)
    following = row_copies(streams.at[1], w_next, sems.at[2:6], 4)
    for copy in late + following:
        copy.start()
    whole = kt[...].astype(F32).reshape(H, F, rows)
    dup[:, 0:F] = whole
    dup[:, F : 2 * F] = whole
    low = lanes((SLABS, F, 128)) < 64
    for g in range(GROUPS):
        if g < 2:
            w = w_early[:, g * 256 : (g + 1) * 256]
        else:
            late[g - 2].wait()
            w = w_late[:, (g - 2) * 256 : (g - 1) * 256]
        convolve(halo, x, w, taps, 0, g, hold, v_out)
        feats = key_features(kt, dup, g)
        left = right = jnp.zeros((ROWS, 128), F32)
        for c in range(rows // CHUNK):
            at = slice(c * CHUNK, (c + 1) * CHUNK)
            before[c, g, :, :128] = left.astype(BF16)
            before[c, g, :, 128:] = right.astype(BF16)
            state = dot(feats[:, at], v_out[at, g * 256 : (g + 1) * 256])
            state = state.reshape(SLABS, PER, F, 256)
            left += jnp.where(low, state[:, 0, :, :128], state[:, 1, :, :128]).reshape(ROWS, 128)
            right += jnp.where(low, state[:, 2, :, 128:], state[:, 3, :, 128:]).reshape(ROWS, 128)
        flat[g, :, :128] = left.astype(BF16)
        flat[g, :, 128:] = right.astype(BF16)
    split = flat.reshape(n, GROUPS * ROWS // n, 256)
    for m, piece in enumerate(pieces):
        piece[...] = split[lax.rem(place[0] + m, n)]
    for copy in following:
        copy.wait()


def project_values(place, halo, x, w_early, streams, taps, kt, n):
    rows, width = x.shape
    half = streams.shape[2]
    part = GROUPS * ROWS // n
    return pl.pallas_call(
        values_body,
        in_specs=[SM, VM, VM, VM, ANY, VM, VM],
        out_specs=[VM] * (3 + n),
        out_shape=[
            pltpu.VMEM((rows, half), BF16),
            pltpu.VMEM((rows // CHUNK, GROUPS, ROWS, 256), BF16),
            pltpu.VMEM((width, half), BF16),
        ]
        + [jax.ShapeDtypeStruct((part, 256), BF16) for _ in range(n)],
        scratch_shapes=[
            pltpu.VMEM((rows + 8, 256), F32),
            pltpu.VMEM((H, 2 * F, rows), F32),
            pltpu.VMEM((GROUPS, ROWS, 256), BF16),
            pltpu.VMEM((width, 512), BF16),
            pltpu.SemaphoreType.DMA((6,)),
        ],
        compiler_params=params(20),
        name="project_values",
    )(place, halo, x, w_early, streams, taps, kt)


def stream_body(stream, halo, x, w, taps, following, out, w_next, hold, sems):
    source = following.at[stream + 1] if len(following.shape) == 3 else following
    copies = row_copies(source, w_next, sems, 4)
    for copy in copies:
        copy.start()
    for j in range(w.shape[1] // 256):
        convolve(halo, x, w[:, j * 256 : (j + 1) * 256], taps, stream, j, hold, out)
    for copy in copies:
        copy.wait()


def project_stream(stream, halo, x, w, taps, following):
    rows = x.shape[0]
    return pl.pallas_call(
        functools.partial(stream_body, stream),
        in_specs=[VM, VM, VM, VM, ANY],
        out_specs=[VM] * 2,
        out_shape=[
            pltpu.VMEM((rows, w.shape[1]), BF16),
            pltpu.VMEM(following.shape[-2:], BF16),
        ],
        scratch_shapes=[pltpu.VMEM((rows + 8, 256), F32), pltpu.SemaphoreType.DMA((4,))],
        compiler_params=params(16),
        name="project_gate" if stream == 1 else "project_skip",
    )(halo, x, w, taps, following)


def inside_body(after, q, kt, v, out):
    low = lanes((CHUNK, 128)) < 64
    head = lanes((CHUNK, 128)) // F
    causal = lax.broadcasted_iota(jnp.int32, (CHUNK, CHUNK), 0) >= lanes((CHUNK, CHUNK))
    for c in range(q.shape[0] // CHUNK):
        rows = slice(c * CHUNK, (c + 1) * CHUNK)
        for part in range(2):
            query = q[rows, part * 128 : (part + 1) * 128] * 0.25
            stacked = jnp.concatenate(
                [jnp.where(head == h, query, 0.0).astype(BF16) for h in range(8)], axis=0
            )
            score = dot(stacked, kt[part * 128 : (part + 1) * 128, rows])
            for pair in range(4):
                both = []
                at = part * 512 + pair * 128
                for h in (2 * pair, 2 * pair + 1):
                    x = score[h * CHUNK : (h + 1) * CHUNK]
                    poly = x * (0.5 * x + 1.0) + 1.0
                    weight = jnp.where(causal, poly, 0.0).astype(BF16)
                    both.append(dot(weight, v[rows, at : at + 128]))
                out[rows, at : at + 128] = jnp.where(low, both[0], both[1])


def inside(after, q, kt, v):
    return pl.pallas_call(
        inside_body,
        in_specs=[ANY, VM, VM, VM],
        out_specs=VM,
        out_shape=pltpu.VMEM(v.shape, F32),
        compiler_params=params(16),
        name="inside",
    )(after, q, kt, v)


def spread():
    src = lax.broadcasted_iota(jnp.int32, (H * F, GROUPS * WIDE), 0)
    col = lax.broadcasted_iota(jnp.int32, (H * F, GROUPS * WIDE), 1)
    g, rest = col // WIDE, col % WIDE
    slab, h, i = rest // 64, (rest // F) % PER, rest % F
    shift = jnp.where(slab == 9, 0, slab)
    want = g * 64 + h * F + (i + shift) % F
    scale = jnp.where(slab == 0, 1.0 / 32, jnp.where(slab == 9, 0.25, 1.0 / 16))
    scale = jnp.where((slab == 8) & (i >= 8), 0.0, scale)
    second = jnp.where(src == want, scale, 0.0).astype(BF16)
    src = lax.broadcasted_iota(jnp.int32, (H * F, GROUPS * 128), 0)
    col = lax.broadcasted_iota(jnp.int32, (H * F, GROUPS * 128), 1)
    first = jnp.where(src == (col // 128) * 64 + col % 64, 1.0, 0.0).astype(BF16)
    return first, second


def mix(start, base, c, q, att, before, gate, skip, gain, first, second):
    rows = pl.ds(pl.multiple_of((base + c) * CHUNK, CHUNK), CHUNK)
    lane = lanes((CHUNK, 128))
    one = jnp.where((lane < 64) & (lane % F == 8), 1.0, 0.0)
    wide = lanes((SLABS, F, 256)) // 64
    mean = lax.broadcasted_iota(jnp.int32, (256, 256), 0) // 64 == lanes((256, 256)) // 64
    mean = jnp.where(mean, 1.0 / 64, 0.0).astype(BF16)
    query = q[rows]
    lead = dot(query, first[...])
    mixed = []
    for g in range(GROUPS):
        b = dot(query, second[:, g * WIDE : (g + 1) * WIDE])
        a = lead[:, g * 128 : (g + 1) * 128]
        feats = [(a * b[:, s * 128 : (s + 1) * 128]).astype(BF16) for s in range(4)]
        b4 = b[:, 512:640]
        feats.append((jnp.where(lane < 64, a * b4, b4) + one).astype(BF16))
        state = (start[g].astype(F32) + before[base + c, g].astype(F32)).astype(BF16)
        state = state.reshape(SLABS, F, 256)
        state = jnp.stack([jnp.where(wide == h, state, 0.0).astype(BF16) for h in range(PER)], axis=1)
        at = slice(g * 256, (g + 1) * 256)
        whole = att[rows, at] + dot(jnp.concatenate(feats, axis=1), state.reshape(WIDE, 256))
        mean_sq = dot((whole * whole).astype(BF16), mean)
        normed = (whole * lax.rsqrt(mean_sq + EPS)).astype(BF16).astype(F32)
        gates = gate[rows, at].astype(F32)
        act = 0.5 * gates * (1.0 + jnp.tanh(0.5 * gates))
        mixed.append((act * (normed * gain[:, at] + skip[rows, at].astype(F32))).astype(BF16))
    return mixed


def gather_start(place, pieces, start):
    n = len(pieces)
    split = start.reshape(n, GROUPS * ROWS // n, 256)
    for m, piece in enumerate(pieces):
        split[lax.rem(place[0] + n - m, n)] = piece[...]


def away_body(place, q, att, before, gate, skip, gain, first, second, w_o, *rest):
    pieces, (out, start, mixed) = rest[:-3], rest[-3:]
    gather_start(place, pieces, start)
    for c in range(out.shape[0] // CHUNK):
        rows = slice(c * CHUNK, (c + 1) * CHUNK)
        made = mix(start, place[1], c, q, att, before, gate, skip, gain, first, second)
        for g in range(GROUPS):
            mixed[rows, g * 256 : (g + 1) * 256] = made[g]
        out[rows] = dot(mixed[rows], w_o[...]).astype(BF16)


def home_body(place, after, q, att, before, gate, skip, gain, first, second, *rest):
    pieces, (mixed, start) = rest[:-2], rest[-2:]
    gather_start(place, pieces, start)
    for c in range(mixed.shape[0] // CHUNK):
        rows = slice(c * CHUNK, (c + 1) * CHUNK)
        made = mix(start, place[2], c, q, att, before, gate, skip, gain, first, second)
        for g in range(GROUPS):
            mixed[rows, g * 256 : (g + 1) * 256] = made[g]


def away(place, tail, w_o, pieces, rows):
    half, width = w_o.shape
    return pl.pallas_call(
        away_body,
        in_specs=[SM] + [VM] * (9 + len(pieces)),
        out_specs=VM,
        out_shape=jax.ShapeDtypeStruct((rows, width), BF16),
        scratch_shapes=[pltpu.VMEM((GROUPS, ROWS, 256), BF16), pltpu.VMEM((rows, half), BF16)],
        compiler_params=params(16),
        name="away",
    )(place, *tail, w_o, *pieces)


def home(place, after, tail, pieces, rows, half):
    return pl.pallas_call(
        home_body,
        in_specs=[SM, ANY] + [VM] * (8 + len(pieces)),
        out_specs=VM,
        out_shape=pltpu.VMEM((rows, half), BF16),
        scratch_shapes=[pltpu.VMEM((GROUPS, ROWS, 256), BF16)],
        compiler_params=params(16),
        name="home",
    )(place, after, *tail, *pieces)


def join_body(mixed, w_o, other, out):
    for j in range(0, out.shape[1], 512):
        own = dot(mixed[...], w_o[:, j : j + 512]).astype(BF16).astype(F32)
        out[:, j : j + 512] = (own + other[:, j : j + 512].astype(F32)).astype(BF16)


def join(mixed, w_o, other):
    return pl.pallas_call(
        join_body,
        grid=(1,),
        in_specs=[VM, VM, pl.BlockSpec(other.shape, lambda i: (0, 0))],
        out_specs=pl.BlockSpec(other.shape, lambda i: (0, 0)),
        out_shape=jax.ShapeDtypeStruct(other.shape, BF16),
        compiler_params=params(16),
        name="join",
    )(mixed, w_o, other)


def shift(block, axes, distance, size):
    return lax.ppermute(block, axes, [(i, i + distance) for i in range(size - distance)])


def turn(block, axis, distance, size):
    return lax.ppermute(block, axis, [(i, (i + distance) % size) for i in range(size)])


def per_device(tokens, w_in, conv_w, w_q, w_k, gain, w_o):
    rows, width = tokens.shape
    half = w_in.shape[3]
    n, blocks = lax.axis_size("ctx"), lax.axis_size("chain")
    me, core = lax.axis_index("ctx"), lax.axis_index("tp")
    per_half = rows // CHUNK // 2
    place = jnp.stack([me, (1 - core) * per_half, core * per_half]).astype(jnp.int32)
    streams = in_hbm(w_in.transpose(1, 2, 0, 3).reshape(3, width, half))
    taps = conv_w.reshape(3, 3, half)
    first, second = spread()

    halo = shift(tokens[rows - 8 :], ("chain", "ctx"), 1, n * blocks)
    q, kt, x, w_early = project_qk(tokens, w_q, w_k, streams)
    values, before, w_gate, *mine = project_values(place, halo, x, w_early, streams, taps, kt, n)
    theirs = [mine[0]] + [turn(mine[m], "ctx", m, n) for m in range(1, n)]
    gate, w_skip = project_stream(1, halo, x, w_gate, taps, streams)
    theirs, gate = lax.optimization_barrier((theirs, gate))
    wide = [t.astype(F32) for t in theirs]
    total = sum(wide).astype(BF16)
    earlier = [shift(total, "chain", d, blocks) for d in range(1, blocks)]
    skip, weight = project_stream(2, halo, x, w_skip, taps, in_hbm(w_o.reshape(half, width)))
    earlier, skip = lax.optimization_barrier((earlier, skip))
    base = sum(e.astype(F32) for e in earlier)
    starts = []
    for m in range(n):
        peer = (me + m) % n
        found = base
        for k, part in enumerate(wide):
            found = found + jnp.where((me - k) % n < peer, part, 0.0)
        starts.append(found.astype(BF16))
    got = [starts[0]] + [turn(starts[m], "ctx", m, n) for m in range(1, n)]
    att = inside(starts[0], q, kt, values)
    got, att = lax.optimization_barrier((got, att))
    tail = (q, att, before, gate, skip, gain, first, second)
    sent = away(place, tail, weight, got, rows // 2)
    swapped = lax.ppermute(sent, "tp", [(0, 1), (1, 0)])
    mixed = home(place, sent, tail, got, rows // 2, half)
    return join(mixed, weight, swapped)


def solution(mesh):
    return jax.shard_map(
        per_device,
        mesh=mesh,
        in_specs=(
            P(("chain", "ctx"), None),
            P(None, None, "tp", None),
            P(None, None, "tp", None),
            P(),
            P(),
            P("tp", None),
            P("tp", None, None),
        ),
        out_specs=P(("chain", "ctx", "tp"), None),
        check_vma=False,
    )
```

```python
import functools

import jax
import jax.numpy as jnp
from jax import lax
from jax.experimental import pallas as pl
from jax.experimental.pallas import tpu as pltpu
from jax.sharding import PartitionSpec as P

H = 16
F = 16
EPS = 1e-05
CHUNK = 256
GROUPS = 4
PER = H // GROUPS
SLABS = 10
ROWS = SLABS * F
WIDE = SLABS * PER * F
F32 = jnp.float32
BF16 = jnp.bfloat16
MIB = 1 << 20


VM = pl.BlockSpec(memory_space=pltpu.VMEM)
ANY = pl.BlockSpec(memory_space=pl.ANY)
SM = pl.BlockSpec(memory_space=pltpu.SMEM)


def params(mib):
    return pltpu.CompilerParams(vmem_limit_bytes=mib * MIB)


def in_hbm(x):
    return pltpu.with_memory_space_constraint(x, pltpu.HBM)


def columns(src, dst, sems, first, count, at=0):
    return [
        pltpu.make_async_copy(
            src.at[:, (first + j) * 256 : (first + j + 1) * 256],
            dst.at[:, (at + j) * 256 : (at + j + 1) * 256],
            sems.at[j],
        )
        for j in range(count)
    ]


def row_copies(src, dst, sems, count):
    size = dst.shape[0] // count
    return [
        pltpu.make_async_copy(
            src.at[i * size : (i + 1) * size], dst.at[i * size : (i + 1) * size], sems.at[i]
        )
        for i in range(count)
    ]


def dot(a, b):
    return jnp.dot(a, b, preferred_element_type=F32)


def lanes(shape):
    return lax.broadcasted_iota(jnp.int32, shape, len(shape) - 1)


def tile(j, size=256):
    return pl.ds(pl.multiple_of(j * size, size), size)


def qk_body(x, wq, wk, taps, streams, q_out, kt_out, x_out, taps_out, w_out, wqk, sems):
    feats = wq.shape[1]
    w_copies = [
        pltpu.make_async_copy(wq, wqk.at[:, 0:feats], sems.at[0]),
        pltpu.make_async_copy(wk, wqk.at[:, feats : 2 * feats], sems.at[1]),
    ]
    x_copies = row_copies(x, x_out, sems.at[2:6], 4)
    later = columns(streams.at[0], w_out, sems.at[6:8], 0, 2)
    later.append(pltpu.make_async_copy(taps, taps_out, sems.at[8]))
    for copy in w_copies + x_copies + later:
        copy.start()
    for copy in w_copies:
        copy.wait()
    size = x.shape[0] // 4
    for i, copy in enumerate(x_copies):
        copy.wait()
        at = slice(i * size, (i + 1) * size)
        both = dot(x_out[at], wqk[...]).astype(BF16)
        q_out[at] = both[:, :feats]
        kt_out[:, at] = both[:, feats:].astype(F32).T.astype(BF16)
    for copy in later:
        copy.wait()


def project_qk(tokens, w_q, w_k, conv_w, streams):
    rows, width = tokens.shape
    feats = w_q.shape[1]
    return pl.pallas_call(
        qk_body,
        in_specs=[ANY] * 5,
        out_specs=[VM] * 5,
        out_shape=[
            pltpu.VMEM((rows, feats), BF16),
            pltpu.VMEM((feats, rows), BF16),
            pltpu.VMEM((rows, width), BF16),
            pltpu.VMEM(conv_w.shape, F32),
            pltpu.VMEM((width, 512), BF16),
        ],
        scratch_shapes=[pltpu.VMEM((width, 2 * feats), BF16), pltpu.SemaphoreType.DMA((9,))],
        compiler_params=params(16),
        name="project_qk",
    )(in_hbm(tokens), in_hbm(w_q), in_hbm(w_k), in_hbm(conv_w), streams)


def convolve(halo, x, w, taps, stream, j, hold, out):
    rows = x.shape[0]
    at = tile(j)
    hold[0:8] = dot(halo[...], w).astype(BF16).astype(F32)
    for a in range(0, rows, 256):
        hold[8 + a : 264 + a] = dot(x[a : a + 256], w).astype(BF16).astype(F32)
    for a in range(0, rows, 256):
        out[a : a + 256, at] = (
            taps[0, stream, :, at] * hold[8 + a : 264 + a]
            + taps[1, stream, :, at] * hold[7 + a : 263 + a]
            + taps[2, stream, :, at] * hold[6 + a : 262 + a]
        ).astype(BF16)


def key_features(kt, dup, g):
    size = kt.shape[1]
    heads = pl.ds(g * PER, PER)
    own = dup[heads, 0:F]
    slabs = [(own * dup[heads, r : r + F]).astype(BF16) for r in range(8)]
    row = lax.broadcasted_iota(jnp.int32, own.shape, 1)
    last = jnp.where(row < 8, own * dup[heads, 8 : 8 + F], 0.0)
    slabs.append(jnp.where(row == 8, 1.0, last).astype(BF16))
    slabs.append(kt[tile(g, 64)].reshape(PER, F, size))
    return jnp.concatenate([s.reshape(PER * F, size) for s in slabs], axis=0)


def values_body(place, halo_in, x, w_early, streams, taps, kt, v_out, before, halo, w_next, *rest):
    pieces, (hold, dup, flat, w_late, sems) = rest[:-5], rest[-5:]
    n = len(pieces)
    rows = x.shape[0]
    ahead = pltpu.make_async_copy(halo_in, halo, sems.at[6])
    late = columns(streams.at[0], w_late, sems.at[0:2], 2, 2)
    following = row_copies(streams.at[1], w_next, sems.at[2:6], 4)
    for copy in [ahead] + late + following:
        copy.start()
    whole = kt[...].astype(F32).reshape(H, F, rows)
    dup[:, 0:F] = whole
    dup[:, F : 2 * F] = whole
    low = lanes((SLABS, F, 128)) < 64
    ahead.wait()

    def group(w_ref, first, j, carry):
        g = first + j
        convolve(halo, x, w_ref[:, tile(j)], taps, 0, g, hold, v_out)
        feats = key_features(kt, dup, g)
        left = right = jnp.zeros((ROWS, 128), F32)
        for c in range(rows // CHUNK):
            at = slice(c * CHUNK, (c + 1) * CHUNK)
            before[c, g, :, :128] = left.astype(BF16)
            before[c, g, :, 128:] = right.astype(BF16)
            state = dot(feats[:, at], v_out[at, tile(g)])
            state = state.reshape(SLABS, PER, F, 256)
            left += jnp.where(low, state[:, 0, :, :128], state[:, 1, :, :128]).reshape(ROWS, 128)
            right += jnp.where(low, state[:, 2, :, 128:], state[:, 3, :, 128:]).reshape(ROWS, 128)
        flat[g, :, :128] = left.astype(BF16)
        flat[g, :, 128:] = right.astype(BF16)
        return carry

    lax.fori_loop(0, 2, functools.partial(group, w_early, 0), 0)
    for copy in late:
        copy.wait()
    lax.fori_loop(0, 2, functools.partial(group, w_late, 2), 0)
    split = flat.reshape(n, GROUPS * ROWS // n, 256)
    for m, piece in enumerate(pieces):
        piece[...] = split[lax.rem(place[0] + m, n)]
    for copy in following:
        copy.wait()


def project_values(place, halo, x, w_early, streams, taps, kt, n):
    rows, width = x.shape
    half = streams.shape[2]
    part = GROUPS * ROWS // n
    return pl.pallas_call(
        values_body,
        in_specs=[SM, ANY, VM, VM, ANY, VM, VM],
        out_specs=[VM] * (4 + n),
        out_shape=[
            pltpu.VMEM((rows, half), BF16),
            pltpu.VMEM((rows // CHUNK, GROUPS, ROWS, 256), BF16),
            pltpu.VMEM(halo.shape, BF16),
            pltpu.VMEM((width, half), BF16),
        ]
        + [jax.ShapeDtypeStruct((part, 256), BF16) for _ in range(n)],
        scratch_shapes=[
            pltpu.VMEM((rows + 8, 256), F32),
            pltpu.VMEM((H, 2 * F, rows), F32),
            pltpu.VMEM((GROUPS, ROWS, 256), BF16),
            pltpu.VMEM((width, 512), BF16),
            pltpu.SemaphoreType.DMA((7,)),
        ],
        compiler_params=params(20),
        name="project_values",
    )(place, halo, x, w_early, streams, taps, kt)


def gate_body(halo, x, w, taps, streams, out, w_next, hold, sems):
    copies = row_copies(streams.at[2], w_next, sems, 4)
    for copy in copies:
        copy.start()

    def step(j, carry):
        convolve(halo, x, w[:, tile(j)], taps, 1, j, hold, out)
        return carry

    lax.fori_loop(0, w.shape[1] // 256, step, 0)
    for copy in copies:
        copy.wait()


def project_gate(halo, x, w, taps, streams):
    rows = x.shape[0]
    return pl.pallas_call(
        gate_body,
        in_specs=[VM, VM, VM, VM, ANY],
        out_specs=[VM] * 2,
        out_shape=[pltpu.VMEM((rows, w.shape[1]), BF16), pltpu.VMEM(w.shape, BF16)],
        scratch_shapes=[pltpu.VMEM((rows + 8, 256), F32), pltpu.SemaphoreType.DMA((4,))],
        compiler_params=params(16),
        name="project_gate",
    )(halo, x, w, taps, streams)


def skip_body(halo, x, w, taps, w_o, gain, out, w_next, gain_out, choose, hold, sems):
    copies = row_copies(w_o, w_next, sems.at[0:4], 4)
    copies.append(pltpu.make_async_copy(gain, gain_out, sems.at[4]))
    for copy in copies:
        copy.start()
    for parity in range(2):
        choose[parity] = selection(parity)

    def step(j, carry):
        convolve(halo, x, w[:, tile(j)], taps, 2, j, hold, out)
        return carry

    lax.fori_loop(0, w.shape[1] // 256, step, 0)
    for copy in copies:
        copy.wait()


def project_skip(halo, x, w, taps, w_o, gain):
    rows = x.shape[0]
    return pl.pallas_call(
        skip_body,
        in_specs=[VM, VM, VM, VM, ANY, ANY],
        out_specs=[VM] * 4,
        out_shape=[
            pltpu.VMEM((rows, w.shape[1]), BF16),
            pltpu.VMEM(w_o.shape, BF16),
            pltpu.VMEM(gain.shape, F32),
            pltpu.VMEM((2, 128, WIDE + 128), BF16),
        ],
        scratch_shapes=[pltpu.VMEM((rows + 8, 256), F32), pltpu.SemaphoreType.DMA((5,))],
        compiler_params=params(16),
        name="project_skip",
    )(halo, x, w, taps, w_o, gain)


def total_body(*refs):
    found = refs[0][...].astype(F32)
    for part in refs[1:-1]:
        found += part[...].astype(F32)
    refs[-1][...] = found.astype(BF16)


def add_up(parts):
    return pl.pallas_call(
        total_body,
        in_specs=[VM] * len(parts),
        out_specs=VM,
        out_shape=jax.ShapeDtypeStruct(parts[0].shape, BF16),
        compiler_params=params(8),
        name="add_up",
    )(*parts)


def starts_body(n, place, *refs):
    parts, earlier, outs, hold = refs[:n], refs[n : -n - 1], refs[-n - 1 : -1], refs[-1]
    for k, part in enumerate(parts):
        hold[lax.rem(place[0] + n - k, n)] = part[...].astype(F32)
    found = jnp.zeros(parts[0].shape, F32)
    for d, block in enumerate(earlier):
        found += jnp.where(place[3] > d, block[...].astype(F32), 0.0)
    for p in range(n):
        own = hold[p]
        hold[p] = found
        found += own
    for m, out in enumerate(outs):
        out[...] = hold[lax.rem(place[0] + m, n)].astype(BF16)


def start_states(place, parts, earlier):
    n, shape = len(parts), parts[0].shape
    return pl.pallas_call(
        functools.partial(starts_body, n),
        in_specs=[SM] + [VM] * (n + len(earlier)),
        out_specs=[VM] * n,
        out_shape=[jax.ShapeDtypeStruct(shape, BF16) for _ in range(n)],
        scratch_shapes=[pltpu.VMEM((n,) + shape, F32)],
        compiler_params=params(8),
        name="start_states",
    )(place, *parts, *earlier)


def inside_body(after, q, kt, v, out):
    low = lanes((CHUNK, 128)) < 64
    head = lanes((CHUNK, 128)) // F
    causal = lax.broadcasted_iota(jnp.int32, (CHUNK, CHUNK), 0) >= lanes((CHUNK, CHUNK))

    def chunk(c, carry):
        rows = tile(c, CHUNK)
        for part in range(2):
            query = q[rows, part * 128 : (part + 1) * 128] * 0.25
            stacked = jnp.concatenate(
                [jnp.where(head == h, query, 0.0).astype(BF16) for h in range(8)], axis=0
            )
            score = dot(stacked, kt[part * 128 : (part + 1) * 128, rows])
            for pair in range(4):
                both = []
                at = part * 512 + pair * 128
                for h in (2 * pair, 2 * pair + 1):
                    x = score[h * CHUNK : (h + 1) * CHUNK]
                    poly = x * (0.5 * x + 1.0) + 1.0
                    weight = jnp.where(causal, poly, 0.0).astype(BF16)
                    both.append(dot(weight, v[rows, at : at + 128]))
                out[rows, at : at + 128] = jnp.where(low, both[0], both[1])
        return carry

    lax.fori_loop(0, q.shape[0] // CHUNK, chunk, 0)


def inside(after, q, kt, v):
    return pl.pallas_call(
        inside_body,
        in_specs=[ANY, VM, VM, VM],
        out_specs=VM,
        out_shape=pltpu.VMEM(v.shape, F32),
        compiler_params=params(16),
        name="inside",
    )(after, q, kt, v)


def selection(parity):
    shape = (128, WIDE + 128)
    src = lax.broadcasted_iota(jnp.int32, shape, 0)
    col = lanes(shape)
    slab, h, i = col // 64, (col // F) % PER, col % F
    turn_by = jnp.where(slab < 9, slab, 0)
    want = parity * 64 + h * F + (i + turn_by) % F
    scale = jnp.where(slab == 0, 1.0 / 32, jnp.where(slab < 9, 1.0 / 16, 0.25))
    scale = jnp.where(slab > 9, 1.0, scale)
    scale = jnp.where((slab == 8) & (i >= 8), 0.0, scale)
    return jnp.where(src == want, scale, 0.0).astype(BF16)


def mix(start, base, c, q, att, before, gate, skip, gain, choose, mixed):
    rows = tile(base + c, CHUNK)
    lane = lanes((CHUNK, 128))
    one = jnp.where((lane < 64) & (lane % F == 8), 1.0, 0.0)
    wide = lanes((SLABS, F, 256)) // 64
    mean = lax.broadcasted_iota(jnp.int32, (256, 256), 0) // 64 == lanes((256, 256)) // 64
    mean = jnp.where(mean, 1.0 / 64, 0.0).astype(BF16)
    for g in range(GROUPS):
        query = q[rows, g // 2 * 128 : g // 2 * 128 + 128]
        b = dot(query, choose[g % 2])
        a = b[:, WIDE:]
        feats = [(a * b[:, s * 128 : (s + 1) * 128]).astype(BF16) for s in range(4)]
        b4 = b[:, 512:640]
        feats.append((jnp.where(lane < 64, a * b4, b4) + one).astype(BF16))
        state = (start[g].astype(F32) + before[base + c, g].astype(F32)).astype(BF16)
        state = state.reshape(SLABS, F, 256)
        state = jnp.stack([jnp.where(wide == h, state, 0.0).astype(BF16) for h in range(PER)], axis=1)
        at = slice(g * 256, (g + 1) * 256)
        whole = att[rows, at] + dot(jnp.concatenate(feats, axis=1), state.reshape(WIDE, 256))
        mean_sq = dot((whole * whole).astype(BF16), mean)
        normed = (whole * lax.rsqrt(mean_sq + EPS)).astype(BF16).astype(F32)
        gates = gate[rows, at].astype(F32)
        act = 0.5 * gates * (1.0 + jnp.tanh(0.5 * gates))
        made = act * (normed * gain[:, at] + skip[rows, at].astype(F32))
        mixed[tile(c, CHUNK), at] = made.astype(BF16)


def gather_start(place, pieces, start):
    n = len(pieces)
    split = start.reshape(n, GROUPS * ROWS // n, 256)
    for m, piece in enumerate(pieces):
        split[lax.rem(place[0] + n - m, n)] = piece[...]


def away_body(place, q, att, before, gate, skip, gain, choose, w_o, *rest):
    pieces, (out, start, mixed) = rest[:-3], rest[-3:]
    gather_start(place, pieces, start)

    def chunk(c, carry):
        mix(start, place[1], c, q, att, before, gate, skip, gain, choose, mixed)
        return carry

    lax.fori_loop(0, out.shape[0] // CHUNK, chunk, 0)

    def columns_of(j, carry):
        out[:, tile(j, 512)] = dot(mixed[...], w_o[:, tile(j, 512)]).astype(BF16)
        return carry

    lax.fori_loop(0, out.shape[1] // 512, columns_of, 0)


def home_body(place, after, q, att, before, gate, skip, gain, choose, *rest):
    pieces, (mixed, start) = rest[:-2], rest[-2:]
    gather_start(place, pieces, start)

    def chunk(c, carry):
        mix(start, place[2], c, q, att, before, gate, skip, gain, choose, mixed)
        return carry

    lax.fori_loop(0, mixed.shape[0] // CHUNK, chunk, 0)


def away(place, tail, w_o, pieces, rows):
    half, width = w_o.shape
    return pl.pallas_call(
        away_body,
        in_specs=[SM] + [VM] * (len(tail) + 1 + len(pieces)),
        out_specs=VM,
        out_shape=jax.ShapeDtypeStruct((rows, width), BF16),
        scratch_shapes=[pltpu.VMEM((GROUPS, ROWS, 256), BF16), pltpu.VMEM((rows, half), BF16)],
        compiler_params=params(16),
        name="away",
    )(place, *tail, w_o, *pieces)


def home(place, after, tail, pieces, rows, half):
    return pl.pallas_call(
        home_body,
        in_specs=[SM, ANY] + [VM] * (len(tail) + len(pieces)),
        out_specs=VM,
        out_shape=pltpu.VMEM((rows, half), BF16),
        scratch_shapes=[pltpu.VMEM((GROUPS, ROWS, 256), BF16)],
        compiler_params=params(16),
        name="home",
    )(place, after, *tail, *pieces)


def join_body(mixed, w_o, other, out, hold, sems):
    copies = []
    for j in range(out.shape[1] // 512):
        at = slice(j * 512, (j + 1) * 512)
        own = dot(mixed[...], w_o[:, at]).astype(BF16).astype(F32)
        hold[:, at] = (own + other[:, at].astype(F32)).astype(BF16)
        copies.append(pltpu.make_async_copy(hold.at[:, at], out.at[:, at], sems.at[j]))
        copies[-1].start()
    for copy in copies:
        copy.wait()


def join(mixed, w_o, other):
    return pl.pallas_call(
        join_body,
        in_specs=[VM, VM, VM],
        out_specs=pl.BlockSpec(memory_space=pltpu.HBM),
        out_shape=jax.ShapeDtypeStruct(other.shape, BF16),
        scratch_shapes=[
            pltpu.VMEM(other.shape, BF16),
            pltpu.SemaphoreType.DMA((other.shape[1] // 512,)),
        ],
        compiler_params=params(16),
        name="join",
    )(mixed, w_o, other)


def shift(block, axes, distance, size):
    return lax.ppermute(block, axes, [(i, i + distance) for i in range(size - distance)])


def turn(block, axis, distance, size):
    return lax.ppermute(block, axis, [(i, (i + distance) % size) for i in range(size)])


def per_device(tokens, w_in, conv_w, w_q, w_k, gain, w_o):
    rows, width = tokens.shape
    half = w_in.shape[3]
    n, blocks = lax.axis_size("ctx"), lax.axis_size("chain")
    me, core = lax.axis_index("ctx"), lax.axis_index("tp")
    per_half = rows // CHUNK // 2
    block = lax.axis_index("chain")
    place = jnp.stack([me, (1 - core) * per_half, core * per_half, block]).astype(jnp.int32)
    streams = in_hbm(w_in.transpose(1, 2, 0, 3).reshape(3, width, half))
    w_out = in_hbm(w_o.reshape(half, width))

    halo = shift(tokens[rows - 8 :], ("chain", "ctx"), 1, n * blocks)
    q, kt, x, taps, w_early = project_qk(tokens, w_q, w_k, conv_w, streams)
    values, before, halo, w_gate, *mine = project_values(
        place, in_hbm(halo), x, w_early, streams, taps, kt, n
    )
    theirs = [mine[0]] + [turn(mine[m], "ctx", m, n) for m in range(1, n)]
    gate, w_skip = project_gate(halo, x, w_gate, taps, streams)
    theirs, gate = lax.optimization_barrier((theirs, gate))
    total = add_up(theirs)
    earlier = [turn(total, "chain", d, blocks) for d in range(1, blocks)]
    skip, weight, gains, choose = project_skip(halo, x, w_skip, taps, w_out, in_hbm(gain))
    earlier, skip = lax.optimization_barrier((earlier, skip))
    starts = start_states(place, theirs, earlier)
    got = [starts[0]] + [turn(starts[m], "ctx", m, n) for m in range(1, n)]
    att = inside(starts[0], q, kt, values)
    got, att = lax.optimization_barrier((got, att))
    tail = (q, att, before, gate, skip, gains, choose)
    sent = away(place, tail, weight, got, rows // 2)
    swapped = lax.ppermute(sent, "tp", [(0, 1), (1, 0)])
    mixed = home(place, sent, tail, got, rows // 2, half)
    return join(mixed, weight, swapped)


def solution(mesh):
    return jax.shard_map(
        per_device,
        mesh=mesh,
        in_specs=(
            P(("chain", "ctx"), None),
            P(None, None, "tp", None),
            P(None, None, "tp", None),
            P(),
            P(),
            P("tp", None),
            P("tp", None, None),
        ),
        out_specs=P(("chain", "ctx", "tp"), None),
        check_vma=False,
    )
```

```python
import functools

import jax
import jax.numpy as jnp
from jax import lax
from jax.experimental import pallas as pl
from jax.experimental.pallas import tpu as pltpu
from jax.sharding import PartitionSpec as P

H = 16
F = 16
EPS = 1e-05
CHUNK = 256
GROUPS = 4
PER = H // GROUPS
SLABS = 10
ROWS = SLABS * F
WIDE = SLABS * PER * F
F32 = jnp.float32
BF16 = jnp.bfloat16
MIB = 1 << 20


VM = pl.BlockSpec(memory_space=pltpu.VMEM)
ANY = pl.BlockSpec(memory_space=pl.ANY)
SM = pl.BlockSpec(memory_space=pltpu.SMEM)


def params(mib):
    return pltpu.CompilerParams(vmem_limit_bytes=mib * MIB)


def in_hbm(x):
    return pltpu.with_memory_space_constraint(x, pltpu.HBM)


def columns(src, dst, sems, first, count, at=0):
    return [
        pltpu.make_async_copy(
            src.at[:, (first + j) * 256 : (first + j + 1) * 256],
            dst.at[:, (at + j) * 256 : (at + j + 1) * 256],
            sems.at[j],
        )
        for j in range(count)
    ]


def row_copies(src, dst, sems, count):
    size = dst.shape[0] // count
    return [
        pltpu.make_async_copy(
            src.at[i * size : (i + 1) * size], dst.at[i * size : (i + 1) * size], sems.at[i]
        )
        for i in range(count)
    ]


def dot(a, b):
    return jnp.dot(a, b, preferred_element_type=F32)


def lanes(shape):
    return lax.broadcasted_iota(jnp.int32, shape, len(shape) - 1)


def tile(j, size=256):
    return pl.ds(pl.multiple_of(j * size, size), size)


def qk_body(x, wq, wk, taps, streams, q_out, kt_out, x_out, taps_out, w_out, choose, wqk, sems):
    feats = wq.shape[1]
    w_copies = [
        pltpu.make_async_copy(wq, wqk.at[:, 0:feats], sems.at[0]),
        pltpu.make_async_copy(wk, wqk.at[:, feats : 2 * feats], sems.at[1]),
    ]
    x_copies = row_copies(x, x_out, sems.at[2:6], 4)
    later = columns(streams.at[0], w_out, sems.at[6:8], 0, 2)
    later.append(pltpu.make_async_copy(taps, taps_out, sems.at[8]))
    for copy in w_copies + x_copies:
        copy.start()
    for parity in range(2):
        choose[parity] = selection(parity)
    for copy in w_copies:
        copy.wait()
    size = x.shape[0] // 4
    for i, copy in enumerate(x_copies):
        copy.wait()
        if i == 1:
            for other in later:
                other.start()
        at = slice(i * size, (i + 1) * size)
        both = dot(x_out[at], wqk[...]).astype(BF16)
        q_out[at] = both[:, :feats]
        kt_out[:, at] = both[:, feats:].astype(F32).T.astype(BF16)
    for copy in later:
        copy.wait()


def project_qk(tokens, w_q, w_k, conv_w, streams):
    rows, width = tokens.shape
    feats = w_q.shape[1]
    return pl.pallas_call(
        qk_body,
        in_specs=[ANY] * 5,
        out_specs=[VM] * 6,
        out_shape=[
            pltpu.VMEM((rows, feats), BF16),
            pltpu.VMEM((feats, rows), BF16),
            pltpu.VMEM((rows, width), BF16),
            pltpu.VMEM(conv_w.shape, F32),
            pltpu.VMEM((width, 512), BF16),
            pltpu.VMEM((2, 128, WIDE + 128), BF16),
        ],
        scratch_shapes=[pltpu.VMEM((width, 2 * feats), BF16), pltpu.SemaphoreType.DMA((9,))],
        compiler_params=params(16),
        name="project_qk",
    )(in_hbm(tokens), in_hbm(w_q), in_hbm(w_k), in_hbm(conv_w), streams)


def project(halo, x, w, c, hold):
    if c == 0:
        hold[0:8] = dot(halo[...], w).astype(BF16).astype(F32)
    at = c * CHUNK
    hold[8 + at : 264 + at] = dot(x[at : at + CHUNK], w).astype(BF16).astype(F32)


def filtered(taps, stream, cols, hold, c):
    at = c * CHUNK
    return (
        taps[0, stream, :, cols] * hold[8 + at : 264 + at]
        + taps[1, stream, :, cols] * hold[7 + at : 263 + at]
        + taps[2, stream, :, cols] * hold[6 + at : 262 + at]
    ).astype(BF16)


def cols_of(j):
    return slice(j * 256, (j + 1) * 256)


def two_stages(count, chunks, first, second):
    for j in range(count + 1):
        for c in range(chunks):
            if j < count:
                first(j, c)
            if j > 0:
                second(j - 1, c)


def key_features(kt, dup, g, at):
    heads = slice(g * PER, (g + 1) * PER)
    own = dup[heads, 0:F, at]
    slabs = [(own * dup[heads, r : r + F, at]).astype(BF16) for r in range(8)]
    row = lax.broadcasted_iota(jnp.int32, own.shape, 1)
    last = jnp.where(row < 8, own * dup[heads, 8 : 8 + F, at], 0.0)
    slabs.append(jnp.where(row == 8, 1.0, last).astype(BF16))
    slabs.append(kt[g * 64 : (g + 1) * 64, at].reshape(PER, F, CHUNK))
    return jnp.concatenate([s.reshape(PER * F, CHUNK) for s in slabs], axis=0)


def values_body(place, halo_in, x, w_early, streams, taps, kt, v_out, before, halo, w_next, *rest):
    pieces, (holds, dup, flat, w_late, sems) = rest[:-5], rest[-5:]
    n = len(pieces)
    rows = x.shape[0]
    late = columns(streams.at[0], w_late, sems.at[0:2], 2, 2)
    following = row_copies(streams.at[1], w_next, sems.at[2:6], 4)
    for copy in late + following:
        copy.start()
    halo[...] = halo_in[...]
    whole = kt[...].astype(F32).reshape(H, F, rows)
    dup[:, 0:F] = whole
    dup[:, F : 2 * F] = whole
    low = lanes((SLABS, F, 128)) < 64
    sums = {}

    def first(g, c):
        if g >= 2 and c == 0:
            late[g - 2].wait()
        w = w_early[:, cols_of(g)] if g < 2 else w_late[:, cols_of(g - 2)]
        project(halo, x, w, c, holds.at[g % 2])

    def second(g, c):
        at = slice(c * CHUNK, (c + 1) * CHUNK)
        values = filtered(taps, 0, cols_of(g), holds.at[g % 2], c)
        v_out[at, cols_of(g)] = values
        left, right = sums.pop(g) if c else (jnp.zeros((ROWS, 128), F32),) * 2
        before[c, g, :, :128] = left.astype(BF16)
        before[c, g, :, 128:] = right.astype(BF16)
        state = dot(key_features(kt, dup, g, at), values).reshape(SLABS, PER, F, 256)
        left += jnp.where(low, state[:, 0, :, :128], state[:, 1, :, :128]).reshape(ROWS, 128)
        right += jnp.where(low, state[:, 2, :, 128:], state[:, 3, :, 128:]).reshape(ROWS, 128)
        sums[g] = left, right
        if c == rows // CHUNK - 1:
            flat[g, :, :128] = left.astype(BF16)
            flat[g, :, 128:] = right.astype(BF16)

    two_stages(GROUPS, rows // CHUNK, first, second)
    split = flat.reshape(n, GROUPS * ROWS // n, 256)
    for m, piece in enumerate(pieces):
        piece[...] = split[lax.rem(place[0] + m, n)]
    for copy in following:
        copy.wait()


def project_values(place, halo, x, w_early, streams, taps, kt, n):
    rows, width = x.shape
    half = streams.shape[2]
    part = GROUPS * ROWS // n
    return pl.pallas_call(
        values_body,
        in_specs=[SM, VM, VM, VM, ANY, VM, VM],
        out_specs=[VM] * (4 + n),
        out_shape=[
            pltpu.VMEM((rows, half), BF16),
            pltpu.VMEM((rows // CHUNK, GROUPS, ROWS, 256), BF16),
            pltpu.VMEM(halo.shape, BF16),
            pltpu.VMEM((width, half), BF16),
        ]
        + [jax.ShapeDtypeStruct((part, 256), BF16) for _ in range(n)],
        scratch_shapes=[
            pltpu.VMEM((2, rows + 8, 256), F32),
            pltpu.VMEM((H, 2 * F, rows), F32),
            pltpu.VMEM((GROUPS, ROWS, 256), BF16),
            pltpu.VMEM((width, 512), BF16),
            pltpu.SemaphoreType.DMA((6,)),
        ],
        compiler_params=params(20),
        name="project_values",
    )(place, halo, x, w_early, streams, taps, kt)


def stream(number, halo, x, w, taps, out, hold):
    chunks = x.shape[0] // CHUNK
    for j in range(w.shape[1] // 256):
        for c in range(chunks + 1):
            if c < chunks:
                project(halo, x, w[:, cols_of(j)], c, hold)
            if c > 0:
                at = slice((c - 1) * CHUNK, c * CHUNK)
                out[at, cols_of(j)] = filtered(taps, number, cols_of(j), hold, c - 1)


def gate_body(halo, x, w, taps, streams, out, w_next, hold, sems):
    copies = row_copies(streams.at[2], w_next, sems, 4)
    for copy in copies:
        copy.start()
    stream(1, halo, x, w, taps, out, hold)
    for copy in copies:
        copy.wait()


def project_gate(halo, x, w, taps, streams):
    rows = x.shape[0]
    return pl.pallas_call(
        gate_body,
        in_specs=[VM, VM, VM, VM, ANY],
        out_specs=[VM] * 2,
        out_shape=[pltpu.VMEM((rows, w.shape[1]), BF16), pltpu.VMEM(w.shape, BF16)],
        scratch_shapes=[pltpu.VMEM((rows + 8, 256), F32), pltpu.SemaphoreType.DMA((4,))],
        compiler_params=params(16),
        name="project_gate",
    )(halo, x, w, taps, streams)


def skip_body(halo, x, w, taps, w_o, gain, out, w_next, gain_out, hold, sems):
    copies = row_copies(w_o, w_next, sems.at[0:4], 4)
    copies.append(pltpu.make_async_copy(gain, gain_out, sems.at[4]))
    for copy in copies:
        copy.start()
    stream(2, halo, x, w, taps, out, hold)
    for copy in copies:
        copy.wait()


def project_skip(halo, x, w, taps, w_o, gain):
    rows = x.shape[0]
    return pl.pallas_call(
        skip_body,
        in_specs=[VM, VM, VM, VM, ANY, ANY],
        out_specs=[VM] * 3,
        out_shape=[
            pltpu.VMEM((rows, w.shape[1]), BF16),
            pltpu.VMEM(w_o.shape, BF16),
            pltpu.VMEM(gain.shape, F32),
        ],
        scratch_shapes=[pltpu.VMEM((rows + 8, 256), F32), pltpu.SemaphoreType.DMA((5,))],
        compiler_params=params(16),
        name="project_skip",
    )(halo, x, w, taps, w_o, gain)


def total_body(*refs):
    found = refs[0][...].astype(F32)
    for part in refs[1:-1]:
        found += part[...].astype(F32)
    refs[-1][...] = found.astype(BF16)


def add_up(parts):
    return pl.pallas_call(
        total_body,
        in_specs=[VM] * len(parts),
        out_specs=VM,
        out_shape=jax.ShapeDtypeStruct(parts[0].shape, BF16),
        compiler_params=params(8),
        name="add_up",
    )(*parts)


def starts_body(n, place, *refs):
    parts, earlier, outs, hold = refs[:n], refs[n : -n - 1], refs[-n - 1 : -1], refs[-1]
    for k, part in enumerate(parts):
        hold[lax.rem(place[0] + n - k, n)] = part[...].astype(F32)
    found = jnp.zeros(parts[0].shape, F32)
    for d, block in enumerate(earlier):
        found += jnp.where(place[3] > d, block[...].astype(F32), 0.0)
    for p in range(n):
        own = hold[p]
        hold[p] = found
        found += own
    for m, out in enumerate(outs):
        out[...] = hold[lax.rem(place[0] + m, n)].astype(BF16)


def start_states(place, parts, earlier):
    n, shape = len(parts), parts[0].shape
    return pl.pallas_call(
        functools.partial(starts_body, n),
        in_specs=[SM] + [VM] * (n + len(earlier)),
        out_specs=[VM] * n,
        out_shape=[jax.ShapeDtypeStruct(shape, BF16) for _ in range(n)],
        scratch_shapes=[pltpu.VMEM((n,) + shape, F32)],
        compiler_params=params(8),
        name="start_states",
    )(place, *parts, *earlier)


def inside_body(after, q, kt, v, out):
    low = lanes((CHUNK, 128)) < 64
    head = lanes((CHUNK, 128)) // F
    causal = lax.broadcasted_iota(jnp.int32, (CHUNK, CHUNK), 0) >= lanes((CHUNK, CHUNK))

    def chunk(c, carry):
        rows = tile(c, CHUNK)
        scores = []
        for part in range(2):
            query = q[rows, part * 128 : (part + 1) * 128] * 0.25
            stacked = jnp.concatenate(
                [jnp.where(head == h, query, 0.0).astype(BF16) for h in range(8)], axis=0
            )
            scores.append(dot(stacked, kt[part * 128 : (part + 1) * 128, rows]))

        def weight(h):
            x = scores[h // 8][h % 8 * CHUNK : (h % 8 + 1) * CHUNK]
            poly = x * (0.5 * x + 1.0) + 1.0
            return jnp.where(causal, poly, 0.0).astype(BF16)

        ready = weight(0)
        done = []
        for h in range(H):
            now, ready = ready, weight(h + 1) if h + 1 < H else None
            at = h // 2 * 128
            done.append(dot(now, v[rows, at : at + 128]))
            if h % 2:
                out[rows, at : at + 128] = jnp.where(low, done[h - 1], done[h])
        return carry

    lax.fori_loop(0, q.shape[0] // CHUNK, chunk, 0)


def inside(after, q, kt, v):
    return pl.pallas_call(
        inside_body,
        in_specs=[ANY, VM, VM, VM],
        out_specs=VM,
        out_shape=pltpu.VMEM(v.shape, F32),
        compiler_params=params(16),
        name="inside",
    )(after, q, kt, v)


def selection(parity):
    shape = (128, WIDE + 128)
    src = lax.broadcasted_iota(jnp.int32, shape, 0)
    col = lanes(shape)
    slab, h, i = col // 64, (col // F) % PER, col % F
    turn_by = jnp.where(slab < 9, slab, 0)
    want = parity * 64 + h * F + (i + turn_by) % F
    scale = jnp.where(slab == 0, 1.0 / 32, jnp.where(slab < 9, 1.0 / 16, 0.25))
    scale = jnp.where(slab > 9, 1.0, scale)
    scale = jnp.where((slab == 8) & (i >= 8), 0.0, scale)
    return jnp.where(src == want, scale, 0.0).astype(BF16)


def mix(start, base, chunks, q, att, before, gate, skip, gain, choose, mixed):
    lane = lanes((CHUNK, 128))
    one = jnp.where((lane < 64) & (lane % F == 8), 1.0, 0.0)
    wide = lanes((1, 256)) // 64
    masks = [jnp.where(wide == h, 1.0, 0.0).astype(BF16) for h in range(PER)]
    mean = lax.broadcasted_iota(jnp.int32, (256, 256), 0) // 64 == lanes((256, 256)) // 64
    mean = jnp.where(mean, 1.0 / 64, 0.0).astype(BF16)
    units = [(c, g) for c in range(chunks) for g in range(GROUPS)]
    factors, whole, mean_sq = {}, {}, {}

    def expand(u):
        c, g = units[u]
        query = q[tile(base + c), g // 2 * 128 : g // 2 * 128 + 128]
        factors[u] = dot(query, choose[g % 2])

    def carried(u):
        c, g = units[u]
        b = factors.pop(u)
        a = b[:, WIDE:]
        feats = [(a * b[:, s * 128 : (s + 1) * 128]).astype(BF16) for s in range(4)]
        b4 = b[:, 512:640]
        feats.append((jnp.where(lane < 64, a * b4, b4) + one).astype(BF16))
        state = (start[g].astype(F32) + before[base + c, g].astype(F32)).astype(BF16)
        state = state.reshape(SLABS, F, 256)
        state = jnp.stack([state * mask for mask in masks], axis=1).reshape(WIDE, 256)
        whole[u] = att[tile(base + c), cols_of(g)] + dot(jnp.concatenate(feats, axis=1), state)

    def squares(u):
        mean_sq[u] = dot((whole[u] * whole[u]).astype(BF16), mean)

    def gated(u):
        c, g = units[u]
        rows, at = tile(base + c), cols_of(g)
        normed = (whole.pop(u) * lax.rsqrt(mean_sq.pop(u) + EPS)).astype(BF16).astype(F32)
        gates = gate[rows, at].astype(F32)
        act = 0.5 * gates * (1.0 + jnp.tanh(0.5 * gates))
        made = act * (normed * gain[:, at] + skip[rows, at].astype(F32))
        mixed[c * CHUNK : (c + 1) * CHUNK, at] = made.astype(BF16)

    for t in range(len(units) + 3):
        for lag, stage in enumerate((expand, carried, squares, gated)):
            if 0 <= t - lag < len(units):
                stage(t - lag)


def gather_start(place, pieces, start):
    n = len(pieces)
    split = start.reshape(n, GROUPS * ROWS // n, 256)
    for m, piece in enumerate(pieces):
        split[lax.rem(place[0] + n - m, n)] = piece[...]


def away_body(place, q, att, before, gate, skip, gain, choose, w_o, *rest):
    pieces, (out, start, mixed) = rest[:-3], rest[-3:]
    gather_start(place, pieces, start)
    chunks = out.shape[0] // CHUNK
    mix(start, place[1], chunks, q, att, before, gate, skip, gain, choose, mixed)

    def columns_of(j, carry):
        out[:, tile(j, 512)] = dot(mixed[...], w_o[:, tile(j, 512)]).astype(BF16)
        return carry

    lax.fori_loop(0, out.shape[1] // 512, columns_of, 0)


def home_body(place, after, q, att, before, gate, skip, gain, choose, *rest):
    pieces, (mixed, start) = rest[:-2], rest[-2:]
    gather_start(place, pieces, start)
    chunks = mixed.shape[0] // CHUNK
    mix(start, place[2], chunks, q, att, before, gate, skip, gain, choose, mixed)


def away(place, tail, w_o, pieces, rows):
    half, width = w_o.shape
    return pl.pallas_call(
        away_body,
        in_specs=[SM] + [VM] * (len(tail) + 1 + len(pieces)),
        out_specs=VM,
        out_shape=jax.ShapeDtypeStruct((rows, width), BF16),
        scratch_shapes=[pltpu.VMEM((GROUPS, ROWS, 256), BF16), pltpu.VMEM((rows, half), BF16)],
        compiler_params=params(16),
        name="away",
    )(place, *tail, w_o, *pieces)


def home(place, after, tail, pieces, rows, half):
    return pl.pallas_call(
        home_body,
        in_specs=[SM, ANY] + [VM] * (len(tail) + len(pieces)),
        out_specs=VM,
        out_shape=pltpu.VMEM((rows, half), BF16),
        scratch_shapes=[pltpu.VMEM((GROUPS, ROWS, 256), BF16)],
        compiler_params=params(16),
        name="home",
    )(place, after, *tail, *pieces)


def join_body(mixed, w_o, other, out, hold, sems):
    copies = []
    for j in range(out.shape[1] // 512):
        at = slice(j * 512, (j + 1) * 512)
        own = dot(mixed[...], w_o[:, at]).astype(BF16).astype(F32)
        hold[:, at] = (own + other[:, at].astype(F32)).astype(BF16)
        copies.append(pltpu.make_async_copy(hold.at[:, at], out.at[:, at], sems.at[j]))
        copies[-1].start()
    for copy in copies:
        copy.wait()


def join(mixed, w_o, other):
    return pl.pallas_call(
        join_body,
        in_specs=[VM, VM, VM],
        out_specs=pl.BlockSpec(memory_space=pltpu.HBM),
        out_shape=jax.ShapeDtypeStruct(other.shape, BF16),
        scratch_shapes=[
            pltpu.VMEM(other.shape, BF16),
            pltpu.SemaphoreType.DMA((other.shape[1] // 512,)),
        ],
        compiler_params=params(16),
        name="join",
    )(mixed, w_o, other)


def shift(block, axes, distance, size):
    return lax.ppermute(block, axes, [(i, i + distance) for i in range(size - distance)])


def turn(block, axis, distance, size):
    return lax.ppermute(block, axis, [(i, (i + distance) % size) for i in range(size)])


def per_device(tokens, w_in, conv_w, w_q, w_k, gain, w_o):
    rows, width = tokens.shape
    half = w_in.shape[3]
    n, blocks = lax.axis_size("ctx"), lax.axis_size("chain")
    me, core = lax.axis_index("ctx"), lax.axis_index("tp")
    per_half = rows // CHUNK // 2
    block = lax.axis_index("chain")
    place = jnp.stack([me, (1 - core) * per_half, core * per_half, block]).astype(jnp.int32)
    streams = in_hbm(w_in.transpose(1, 2, 0, 3).reshape(3, width, half))
    w_out = in_hbm(w_o.reshape(half, width))

    halo = shift(tokens[rows - 8 :], ("chain", "ctx"), 1, n * blocks)
    q, kt, x, taps, w_early, choose = project_qk(tokens, w_q, w_k, conv_w, streams)
    values, before, halo, w_gate, *mine = project_values(
        place, halo, x, w_early, streams, taps, kt, n
    )
    theirs = [mine[0]] + [turn(mine[m], "ctx", m, n) for m in range(1, n)]
    gate, w_skip = project_gate(halo, x, w_gate, taps, streams)
    theirs, gate = lax.optimization_barrier((theirs, gate))
    total = add_up(theirs)
    earlier = [turn(total, "chain", d, blocks) for d in range(1, blocks)]
    skip, weight, gains = project_skip(halo, x, w_skip, taps, w_out, in_hbm(gain))
    earlier, skip = lax.optimization_barrier((earlier, skip))
    starts = start_states(place, theirs, earlier)
    got = [starts[0]] + [turn(starts[m], "ctx", m, n) for m in range(1, n)]
    att = inside(starts[0], q, kt, values)
    got, att = lax.optimization_barrier((got, att))
    tail = (q, att, before, gate, skip, gains, choose)
    sent = away(place, tail, weight, got, rows // 2)
    swapped = lax.ppermute(sent, "tp", [(0, 1), (1, 0)])
    mixed = home(place, sent, tail, got, rows // 2, half)
    return join(mixed, weight, swapped)


def solution(mesh):
    return jax.shard_map(
        per_device,
        mesh=mesh,
        in_specs=(
            P(("chain", "ctx"), None),
            P(None, None, "tp", None),
            P(None, None, "tp", None),
            P(),
            P(),
            P("tp", None),
            P("tp", None, None),
        ),
        out_specs=P(("chain", "ctx", "tp"), None),
        check_vma=False,
    )
```

```python
import functools

import jax
import jax.numpy as jnp
from jax import lax
from jax.experimental import pallas as pl
from jax.experimental.pallas import tpu as pltpu
from jax.sharding import PartitionSpec as P

H = 16
F = 16
EPS = 1e-05
CHUNK = 256
GROUPS = 4
PER = H // GROUPS
SLABS = 10
ROWS = SLABS * F
WIDE = SLABS * PER * F
F32 = jnp.float32
BF16 = jnp.bfloat16
MIB = 1 << 20


VM = pl.BlockSpec(memory_space=pltpu.VMEM)
ANY = pl.BlockSpec(memory_space=pl.ANY)
SM = pl.BlockSpec(memory_space=pltpu.SMEM)


def params(mib):
    return pltpu.CompilerParams(vmem_limit_bytes=mib * MIB)


def in_hbm(x):
    return pltpu.with_memory_space_constraint(x, pltpu.HBM)


def half_copy(src, dst, sem, part):
    size = dst.shape[1]
    return pltpu.make_async_copy(src.at[:, part * size : (part + 1) * size], dst, sem)


def row_copies(src, dst, sems, count):
    size = dst.shape[0] // count
    return [
        pltpu.make_async_copy(
            src.at[i * size : (i + 1) * size], dst.at[i * size : (i + 1) * size], sems.at[i]
        )
        for i in range(count)
    ]


def dot(a, b):
    return jnp.dot(a, b, preferred_element_type=F32)


def lanes(shape):
    return lax.broadcasted_iota(jnp.int32, shape, len(shape) - 1)


def tile(j, size=256):
    return pl.ds(pl.multiple_of(j * size, size), size)


def qk_body(x, wq, wk, taps, streams, q_out, kt_out, x_out, taps_out, w_out, choose, wqk, sems):
    feats = wq.shape[1]
    w_copies = [
        pltpu.make_async_copy(wq, wqk.at[:, 0:feats], sems.at[0]),
        pltpu.make_async_copy(wk, wqk.at[:, feats : 2 * feats], sems.at[1]),
    ]
    x_copies = row_copies(x, x_out, sems.at[2:6], 4)
    later = [half_copy(streams.at[0], w_out, sems.at[6], 0)]
    later.append(pltpu.make_async_copy(taps, taps_out, sems.at[7]))
    for copy in w_copies + x_copies:
        copy.start()
    for parity in range(2):
        choose[parity] = selection(parity)
    for copy in w_copies:
        copy.wait()
    w = wqk[...]
    size = x.shape[0] // 4
    for i, copy in enumerate(x_copies):
        copy.wait()
        if i == 1:
            for other in later:
                other.start()
        at = slice(i * size, (i + 1) * size)
        both = dot(x_out[at], w).astype(BF16)
        q_out[at] = both[:, :feats]
        kt_out[:, at] = both[:, feats:].astype(F32).T.astype(BF16)
    for copy in later:
        copy.wait()


def project_qk(tokens, w_q, w_k, conv_w, streams):
    rows, width = tokens.shape
    feats = w_q.shape[1]
    return pl.pallas_call(
        qk_body,
        in_specs=[ANY] * 5,
        out_specs=[VM] * 6,
        out_shape=[
            pltpu.VMEM((rows, feats), BF16),
            pltpu.VMEM((feats, rows), BF16),
            pltpu.VMEM((rows, width), BF16),
            pltpu.VMEM(conv_w.shape, F32),
            pltpu.VMEM((width, 512), BF16),
            pltpu.VMEM((2, 128, WIDE + 128), BF16),
        ],
        scratch_shapes=[
            pltpu.VMEM((width, 2 * feats), BF16),
            pltpu.SemaphoreType.DMA((8,)),
        ],
        compiler_params=params(16),
        name="project_qk",
    )(in_hbm(tokens), in_hbm(w_q), in_hbm(w_k), in_hbm(conv_w), streams)


def project(halo, x, w, c, hold):
    if c == 0:
        hold[0:8] = dot(halo[...], w).astype(BF16).astype(F32)
    at = c * CHUNK
    hold[8 + at : 264 + at] = dot(x[at : at + CHUNK], w).astype(BF16).astype(F32)


def filtered(taps, stream, cols, hold, c):
    at = c * CHUNK
    return (
        taps[0, stream, :, cols] * hold[8 + at : 264 + at]
        + taps[1, stream, :, cols] * hold[7 + at : 263 + at]
        + taps[2, stream, :, cols] * hold[6 + at : 262 + at]
    ).astype(BF16)


def cols_of(j):
    return slice(j * 256, (j + 1) * 256)


def stream_tile(number, j, halo, x, w, taps, out, hold):
    chunks = x.shape[0] // CHUNK
    for c in range(chunks + 1):
        if c < chunks:
            project(halo, x, w, c, hold)
        if c > 0:
            at = slice((c - 1) * CHUNK, c * CHUNK)
            out[at, cols_of(j)] = filtered(taps, number, cols_of(j), hold, c - 1)


def key_features(kt, dup, g, at):
    heads = slice(g * PER, (g + 1) * PER)
    own = dup[heads, 0:F, at]
    slabs = [(own * dup[heads, r : r + F, at]).astype(BF16) for r in range(8)]
    row = lax.broadcasted_iota(jnp.int32, own.shape, 1)
    last = jnp.where(row < 8, own * dup[heads, 8 : 8 + F, at], 0.0)
    slabs.append(jnp.where(row == 8, 1.0, last).astype(BF16))
    slabs.append(kt[g * 64 : (g + 1) * 64, at].reshape(PER, F, CHUNK))
    return jnp.concatenate([s.reshape(PER * F, CHUNK) for s in slabs], axis=0)


def values_body(place, halo_in, x, w_early, streams, taps, kt, v_out, before, halo, w_next, *rest):
    pieces, (holds, dup, flat, w_late, sems) = rest[:-5], rest[-5:]
    n = len(pieces)
    rows = x.shape[0]
    late = half_copy(streams.at[0], w_late, sems.at[0], 1)
    following = row_copies(streams.at[1], w_next, sems.at[1:5], 4)
    for copy in [late] + following:
        copy.start()
    halo[...] = halo_in[...]
    whole = kt[...].astype(F32).reshape(H, F, rows)
    dup[:, 0:F] = whole
    dup[:, F : 2 * F] = whole
    low = lanes((SLABS, F, 128)) < 64
    chunks = [slice(at, at + CHUNK) for at in range(0, rows, CHUNK)]

    def states(g):
        left = right = jnp.zeros((ROWS, 128), F32)
        for c, at in enumerate(chunks):
            before[c, g, :, :128] = left.astype(BF16)
            before[c, g, :, 128:] = right.astype(BF16)
            state = dot(key_features(kt, dup, g, at), v_out[at, cols_of(g)])
            state = state.reshape(SLABS, PER, F, 256)
            left += jnp.where(low, state[:, 0, :, :128], state[:, 1, :, :128]).reshape(ROWS, 128)
            right += jnp.where(low, state[:, 2, :, 128:], state[:, 3, :, 128:]).reshape(ROWS, 128)
        flat[g, :, :128] = left.astype(BF16)
        flat[g, :, 128:] = right.astype(BF16)

    for g in range(GROUPS):
        if g == 2:
            late.wait()
        w = w_early[:, cols_of(g)] if g < 2 else w_late[:, cols_of(g - 2)]
        stream_tile(0, g, halo, x, w, taps, v_out, holds.at[g % 2])
        if g > 0:
            states(g - 1)
    states(GROUPS - 1)
    split = flat.reshape(n, GROUPS * ROWS // n, 256)
    for m, piece in enumerate(pieces):
        piece[...] = split[lax.rem(place[0] + m, n)]
    for copy in following:
        copy.wait()


def project_values(place, halo, x, w_early, streams, taps, kt, n):
    rows, width = x.shape
    half = streams.shape[2]
    part = GROUPS * ROWS // n
    return pl.pallas_call(
        values_body,
        in_specs=[SM, VM, VM, VM, ANY, VM, VM],
        out_specs=[VM] * (4 + n),
        out_shape=[
            pltpu.VMEM((rows, half), BF16),
            pltpu.VMEM((rows // CHUNK, GROUPS, ROWS, 256), BF16),
            pltpu.VMEM(halo.shape, BF16),
            pltpu.VMEM((width, half), BF16),
        ]
        + [jax.ShapeDtypeStruct((part, 256), BF16) for _ in range(n)],
        scratch_shapes=[
            pltpu.VMEM((2, rows + 8, 256), F32),
            pltpu.VMEM((H, 2 * F, rows), F32),
            pltpu.VMEM((GROUPS, ROWS, 256), BF16),
            pltpu.VMEM((width, 512), BF16),
            pltpu.SemaphoreType.DMA((5,)),
        ],
        compiler_params=params(20),
        name="project_values",
    )(place, halo, x, w_early, streams, taps, kt)


def stream(number, halo, x, w, taps, out, hold):
    for j in range(w.shape[1] // 256):
        stream_tile(number, j, halo, x, w[:, cols_of(j)], taps, out, hold)


def gate_body(halo, x, w, taps, streams, out, w_next, hold, sems):
    copies = row_copies(streams.at[2], w_next, sems, 4)
    for copy in copies:
        copy.start()
    stream(1, halo, x, w, taps, out, hold)
    for copy in copies:
        copy.wait()


def project_gate(halo, x, w, taps, streams):
    rows = x.shape[0]
    return pl.pallas_call(
        gate_body,
        in_specs=[VM, VM, VM, VM, ANY],
        out_specs=[VM] * 2,
        out_shape=[pltpu.VMEM((rows, w.shape[1]), BF16), pltpu.VMEM(w.shape, BF16)],
        scratch_shapes=[pltpu.VMEM((rows + 8, 256), F32), pltpu.SemaphoreType.DMA((4,))],
        compiler_params=params(16),
        name="project_gate",
    )(halo, x, w, taps, streams)


def skip_body(halo, x, w, taps, w_o, gain, out, w_next, gain_out, hold, sems):
    copies = row_copies(w_o, w_next, sems.at[0:4], 4)
    copies.append(pltpu.make_async_copy(gain, gain_out, sems.at[4]))
    for copy in copies:
        copy.start()
    stream(2, halo, x, w, taps, out, hold)
    for copy in copies:
        copy.wait()


def project_skip(halo, x, w, taps, w_o, gain):
    rows = x.shape[0]
    return pl.pallas_call(
        skip_body,
        in_specs=[VM, VM, VM, VM, ANY, ANY],
        out_specs=[VM] * 3,
        out_shape=[
            pltpu.VMEM((rows, w.shape[1]), BF16),
            pltpu.VMEM(w_o.shape, BF16),
            pltpu.VMEM(gain.shape, F32),
        ],
        scratch_shapes=[pltpu.VMEM((rows + 8, 256), F32), pltpu.SemaphoreType.DMA((5,))],
        compiler_params=params(16),
        name="project_skip",
    )(halo, x, w, taps, w_o, gain)


def total_body(*refs):
    found = refs[0][...].astype(F32)
    for part in refs[1:-1]:
        found += part[...].astype(F32)
    refs[-1][...] = found.astype(BF16)


def add_up(parts):
    return pl.pallas_call(
        total_body,
        in_specs=[VM] * len(parts),
        out_specs=VM,
        out_shape=jax.ShapeDtypeStruct(parts[0].shape, BF16),
        compiler_params=params(8),
        name="add_up",
    )(*parts)


def starts_body(n, place, *refs):
    parts, earlier, outs, hold = refs[:n], refs[n : -n - 1], refs[-n - 1 : -1], refs[-1]
    for k, part in enumerate(parts):
        hold[lax.rem(place[0] + n - k, n)] = part[...].astype(F32)
    found = jnp.zeros(parts[0].shape, F32)
    for d, block in enumerate(earlier):
        found += jnp.where(place[3] > d, block[...].astype(F32), 0.0)
    for p in range(n):
        own = hold[p]
        hold[p] = found
        found += own
    for m, out in enumerate(outs):
        out[...] = hold[lax.rem(place[0] + m, n)].astype(BF16)


def start_states(place, parts, earlier):
    n, shape = len(parts), parts[0].shape
    return pl.pallas_call(
        functools.partial(starts_body, n),
        in_specs=[SM] + [VM] * (n + len(earlier)),
        out_specs=[VM] * n,
        out_shape=[jax.ShapeDtypeStruct(shape, BF16) for _ in range(n)],
        scratch_shapes=[pltpu.VMEM((n,) + shape, F32)],
        compiler_params=params(8),
        name="start_states",
    )(place, *parts, *earlier)


def inside_body(after, q, kt, v, out):
    low = lanes((CHUNK, 128)) < 64
    head = lanes((CHUNK, 128)) // F
    causal = lax.broadcasted_iota(jnp.int32, (CHUNK, CHUNK), 0) >= lanes((CHUNK, CHUNK))

    def chunk(c, carry):
        rows = tile(c, CHUNK)
        scores = []
        for part in range(2):
            query = q[rows, part * 128 : (part + 1) * 128] * 0.25
            stacked = jnp.concatenate(
                [jnp.where(head == h, query, 0.0).astype(BF16) for h in range(8)], axis=0
            )
            scores.append(dot(stacked, kt[part * 128 : (part + 1) * 128, rows]))

        def weight(h):
            x = scores[h // 8][h % 8 * CHUNK : (h % 8 + 1) * CHUNK]
            poly = x * (0.5 * x + 1.0) + 1.0
            return jnp.where(causal, poly, 0.0).astype(BF16)

        ready = weight(0)
        done = []
        for h in range(H):
            now, ready = ready, weight(h + 1) if h + 1 < H else None
            at = h // 2 * 128
            done.append(dot(now, v[rows, at : at + 128]))
            if h % 2:
                out[rows, at : at + 128] = jnp.where(low, done[h - 1], done[h])
        return carry

    lax.fori_loop(0, q.shape[0] // CHUNK, chunk, 0)


def inside(after, q, kt, v):
    return pl.pallas_call(
        inside_body,
        in_specs=[ANY, VM, VM, VM],
        out_specs=VM,
        out_shape=pltpu.VMEM(v.shape, F32),
        compiler_params=params(16),
        name="inside",
    )(after, q, kt, v)


def selection(parity):
    shape = (128, WIDE + 128)
    src = lax.broadcasted_iota(jnp.int32, shape, 0)
    col = lanes(shape)
    slab, h, i = col // 64, (col // F) % PER, col % F
    turn_by = jnp.where(slab < 9, slab, 0)
    want = parity * 64 + h * F + (i + turn_by) % F
    scale = jnp.where(slab == 0, 1.0 / 32, jnp.where(slab < 9, 1.0 / 16, 0.25))
    scale = jnp.where(slab > 9, 1.0, scale)
    scale = jnp.where((slab == 8) & (i >= 8), 0.0, scale)
    return jnp.where(src == want, scale, 0.0).astype(BF16)


def mix(start, base, chunks, q, att, before, gate, skip, gain, choose, w_o, mixed, out):
    lane = lanes((CHUNK, 128))
    one = jnp.where((lane < 64) & (lane % F == 8), 1.0, 0.0)
    wide = lanes((1, 256)) // 64
    masks = [jnp.where(wide == h, 1.0, 0.0).astype(BF16) for h in range(PER)]
    mean = lax.broadcasted_iota(jnp.int32, (256, 256), 0) // 64 == lanes((256, 256)) // 64
    mean = jnp.where(mean, 1.0 / 64, 0.0).astype(BF16)
    units = [(c, g) for c in range(chunks) for g in range(GROUPS)]
    factors, whole, mean_sq = {}, {}, {}

    def expand(u):
        c, g = units[u]
        query = q[tile(base + c), g // 2 * 128 : g // 2 * 128 + 128]
        factors[u] = dot(query, choose[g % 2])

    def carried(u):
        c, g = units[u]
        b = factors.pop(u)
        a = b[:, WIDE:]
        feats = [(a * b[:, s * 128 : (s + 1) * 128]).astype(BF16) for s in range(4)]
        b4 = b[:, 512:640]
        feats.append((jnp.where(lane < 64, a * b4, b4) + one).astype(BF16))
        state = (start[g].astype(F32) + before[base + c, g].astype(F32)).astype(BF16)
        state = state.reshape(SLABS, F, 256)
        state = jnp.stack([state * mask for mask in masks], axis=1).reshape(WIDE, 256)
        whole[u] = att[tile(base + c), cols_of(g)] + dot(jnp.concatenate(feats, axis=1), state)

    def squares(u):
        mean_sq[u] = dot((whole[u] * whole[u]).astype(BF16), mean)

    def gated(u):
        c, g = units[u]
        rows, at = tile(base + c), cols_of(g)
        normed = (whole.pop(u) * lax.rsqrt(mean_sq.pop(u) + EPS)).astype(BF16).astype(F32)
        gates = gate[rows, at].astype(F32)
        act = 0.5 * gates * (1.0 + jnp.tanh(0.5 * gates))
        made = act * (normed * gain[:, at] + skip[rows, at].astype(F32))
        mixed[c * CHUNK : (c + 1) * CHUNK, at] = made.astype(BF16)

    def product(u):
        c, j = units[u]
        rows, at = slice(c * CHUNK, (c + 1) * CHUNK), slice(j * 512, (j + 1) * 512)
        out[rows, at] = dot(mixed[rows], w_o[:, at]).astype(BF16)

    stages = ((expand, 0), (carried, 1), (squares, 2), (gated, 3), (product, 3 + GROUPS))
    for t in range(len(units) + 3 + GROUPS):
        for stage, lag in stages:
            if 0 <= t - lag < len(units):
                stage(t - lag)


def gather_start(place, pieces, start):
    n = len(pieces)
    split = start.reshape(n, GROUPS * ROWS // n, 256)
    for m, piece in enumerate(pieces):
        split[lax.rem(place[0] + n - m, n)] = piece[...]


def finish_body(which, place, after, q, att, before, gate, skip, gain, choose, w_o, *rest):
    pieces, (out, start, mixed) = rest[:-3], rest[-3:]
    gather_start(place, pieces, start)
    chunks = out.shape[0] // CHUNK
    mix(start, place[which], chunks, q, att, before, gate, skip, gain, choose, w_o, mixed, out)


def finish(which, place, after, tail, w_o, pieces, rows):
    half, width = w_o.shape
    return pl.pallas_call(
        functools.partial(finish_body, which),
        in_specs=[SM, ANY] + [VM] * (len(tail) + 1 + len(pieces)),
        out_specs=VM,
        out_shape=pltpu.VMEM((rows, width), BF16),
        scratch_shapes=[pltpu.VMEM((GROUPS, ROWS, 256), BF16), pltpu.VMEM((rows, half), BF16)],
        compiler_params=params(16),
        name="away" if which == 1 else "home",
    )(place, after, *tail, w_o, *pieces)


def join_body(own, other, out, hold, sems):
    copies = []
    size = out.shape[0] // 8
    for i in range(8):
        at = slice(i * size, (i + 1) * size)
        hold[at] = (own[at].astype(F32) + other[at].astype(F32)).astype(BF16)
        copies.append(pltpu.make_async_copy(hold.at[at], out.at[at], sems.at[i]))
        copies[-1].start()
    for copy in copies:
        copy.wait()


def join(own, other):
    return pl.pallas_call(
        join_body,
        in_specs=[VM, VM],
        out_specs=pl.BlockSpec(memory_space=pltpu.HBM),
        out_shape=jax.ShapeDtypeStruct(other.shape, BF16),
        scratch_shapes=[pltpu.VMEM(other.shape, BF16), pltpu.SemaphoreType.DMA((8,))],
        compiler_params=params(8),
        name="join",
    )(own, other)


def shift(block, axes, distance, size):
    return lax.ppermute(block, axes, [(i, i + distance) for i in range(size - distance)])


def turn(block, axis, distance, size):
    return lax.ppermute(block, axis, [(i, (i + distance) % size) for i in range(size)])


def per_device(tokens, w_in, conv_w, w_q, w_k, gain, w_o):
    rows, width = tokens.shape
    half = w_in.shape[3]
    n, blocks = lax.axis_size("ctx"), lax.axis_size("chain")
    me, core = lax.axis_index("ctx"), lax.axis_index("tp")
    per_half = rows // CHUNK // 2
    block = lax.axis_index("chain")
    place = jnp.stack([me, (1 - core) * per_half, core * per_half, block]).astype(jnp.int32)
    streams = in_hbm(w_in.transpose(1, 2, 0, 3).reshape(3, width, half))
    w_out = in_hbm(w_o.reshape(half, width))

    halo = shift(tokens[rows - 8 :], ("chain", "ctx"), 1, n * blocks)
    q, kt, x, taps, w_early, choose = project_qk(tokens, w_q, w_k, conv_w, streams)
    values, before, halo, w_gate, *mine = project_values(
        place, halo, x, w_early, streams, taps, kt, n
    )
    theirs = [mine[0]] + [turn(mine[m], "ctx", m, n) for m in range(1, n)]
    gate, w_skip = project_gate(halo, x, w_gate, taps, streams)
    theirs, gate = lax.optimization_barrier((theirs, gate))
    total = add_up(theirs)
    earlier = [turn(total, "chain", d, blocks) for d in range(1, blocks)]
    skip, weight, gains = project_skip(halo, x, w_skip, taps, w_out, in_hbm(gain))
    earlier, skip = lax.optimization_barrier((earlier, skip))
    starts = start_states(place, theirs, earlier)
    got = [starts[0]] + [turn(starts[m], "ctx", m, n) for m in range(1, n)]
    att = inside(starts[0], q, kt, values)
    got, att = lax.optimization_barrier((got, att))
    tail = (q, att, before, gate, skip, gains, choose)
    sent = finish(1, place, att, tail, weight, got, rows // 2)
    swapped = lax.ppermute(sent, "tp", [(0, 1), (1, 0)])
    kept = finish(2, place, sent, tail, weight, got, rows // 2)
    return join(kept, swapped)


def solution(mesh):
    return jax.shard_map(
        per_device,
        mesh=mesh,
        in_specs=(
            P(("chain", "ctx"), None),
            P(None, None, "tp", None),
            P(None, None, "tp", None),
            P(),
            P(),
            P("tp", None),
            P("tp", None, None),
        ),
        out_specs=P(("chain", "ctx", "tp"), None),
        check_vma=False,
    )
```

```python
import functools

import jax
import jax.numpy as jnp
from jax import lax
from jax.experimental import pallas as pl
from jax.experimental.pallas import tpu as pltpu
from jax.sharding import PartitionSpec as P

H = 16
F = 16
EPS = 1e-05
CHUNK = 256
GROUPS = 4
PER = H // GROUPS
SLABS = 10
ROWS = SLABS * F
WIDE = SLABS * PER * F
F32 = jnp.float32
BF16 = jnp.bfloat16
MIB = 1 << 20


VM = pl.BlockSpec(memory_space=pltpu.VMEM)
ANY = pl.BlockSpec(memory_space=pl.ANY)


def params(mib):
    return pltpu.CompilerParams(vmem_limit_bytes=mib * MIB)


def in_hbm(x):
    return pltpu.with_memory_space_constraint(x, pltpu.HBM)


def half_copy(src, dst, sem, part):
    size = dst.shape[1]
    return pltpu.make_async_copy(src.at[:, part * size : (part + 1) * size], dst, sem)


def row_copies(src, dst, sems, count):
    size = dst.shape[0] // count
    return [
        pltpu.make_async_copy(
            src.at[i * size : (i + 1) * size], dst.at[i * size : (i + 1) * size], sems.at[i]
        )
        for i in range(count)
    ]


def dot(a, b):
    return jnp.dot(a, b, preferred_element_type=F32)


def lanes(shape):
    return lax.broadcasted_iota(jnp.int32, shape, len(shape) - 1)


def tile(j, size=256):
    return pl.ds(pl.multiple_of(j * size, size), size)


def qk_body(x, wq, wk, taps, streams, q_out, kt_out, x_out, taps_out, w_out, choose, wqk, sems):
    feats = wq.shape[1]
    w_copies = [
        pltpu.make_async_copy(wq, wqk.at[:, 0:feats], sems.at[0]),
        pltpu.make_async_copy(wk, wqk.at[:, feats : 2 * feats], sems.at[1]),
    ]
    x_copies = row_copies(x, x_out, sems.at[2:6], 4)
    later = [half_copy(streams.at[0], w_out, sems.at[6], 0)]
    later.append(pltpu.make_async_copy(taps, taps_out, sems.at[7]))
    for copy in w_copies + x_copies:
        copy.start()
    for parity in range(2):
        choose[parity] = selection(parity)
    for copy in w_copies:
        copy.wait()
    w = wqk[...]
    size = x.shape[0] // 4
    for i, copy in enumerate(x_copies):
        copy.wait()
        if i == 1:
            for other in later:
                other.start()
        at = slice(i * size, (i + 1) * size)
        both = dot(x_out[at], w).astype(BF16)
        q_out[at] = both[:, :feats]
        kt_out[:, at] = both[:, feats:].astype(F32).T.astype(BF16)
    for copy in later:
        copy.wait()


def project_qk(tokens, w_q, w_k, conv_w, streams):
    rows, width = tokens.shape
    feats = w_q.shape[1]
    return pl.pallas_call(
        qk_body,
        in_specs=[ANY] * 5,
        out_specs=[VM] * 6,
        out_shape=[
            pltpu.VMEM((rows, feats), BF16),
            pltpu.VMEM((feats, rows), BF16),
            pltpu.VMEM((rows, width), BF16),
            pltpu.VMEM(conv_w.shape, F32),
            pltpu.VMEM((width, 512), BF16),
            pltpu.VMEM((2, 128, WIDE + 128), BF16),
        ],
        scratch_shapes=[
            pltpu.VMEM((width, 2 * feats), BF16),
            pltpu.SemaphoreType.DMA((8,)),
        ],
        compiler_params=params(16),
        name="project_qk",
    )(in_hbm(tokens), in_hbm(w_q), in_hbm(w_k), in_hbm(conv_w), streams)


def project(halo, x, w, c, hold):
    if c == 0:
        hold[0:8] = dot(halo[...], w).astype(BF16).astype(F32)
    at = c * CHUNK
    hold[8 + at : 264 + at] = dot(x[at : at + CHUNK], w).astype(BF16).astype(F32)


def filtered(taps, stream, cols, hold, c):
    at = c * CHUNK
    return (
        taps[0, stream, :, cols] * hold[8 + at : 264 + at]
        + taps[1, stream, :, cols] * hold[7 + at : 263 + at]
        + taps[2, stream, :, cols] * hold[6 + at : 262 + at]
    ).astype(BF16)


def cols_of(j):
    return slice(j * 256, (j + 1) * 256)


def stream_tile(number, j, halo, x, w, taps, out, hold):
    chunks = x.shape[0] // CHUNK
    for c in range(chunks + 1):
        if c < chunks:
            project(halo, x, w, c, hold)
        if c > 0:
            at = slice((c - 1) * CHUNK, c * CHUNK)
            out[at, cols_of(j)] = filtered(taps, number, cols_of(j), hold, c - 1)


def key_features(kt, dup, g, at):
    heads = slice(g * PER, (g + 1) * PER)
    own = dup[heads, 0:F, at]
    slabs = [(own * dup[heads, r : r + F, at]).astype(BF16) for r in range(8)]
    row = lax.broadcasted_iota(jnp.int32, own.shape, 1)
    last = jnp.where(row < 8, own * dup[heads, 8 : 8 + F, at], 0.0)
    slabs.append(jnp.where(row == 8, 1.0, last).astype(BF16))
    slabs.append(kt[g * 64 : (g + 1) * 64, at].reshape(PER, F, CHUNK))
    return jnp.concatenate([s.reshape(PER * F, CHUNK) for s in slabs], axis=0)


def values_body(halo_in, x, w_early, streams, taps, kt, v_out, before, halo, w_next, *rest):
    pieces, (holds, dup, flat, w_late, sems) = rest[:-5], rest[-5:]
    n = len(pieces)
    rows = x.shape[0]
    late = half_copy(streams.at[0], w_late, sems.at[0], 1)
    following = row_copies(streams.at[1], w_next, sems.at[1:5], 4)
    for copy in [late] + following:
        copy.start()
    halo[...] = halo_in[...]
    whole = kt[...].astype(F32).reshape(H, F, rows)
    dup[:, 0:F] = whole
    dup[:, F : 2 * F] = whole
    low = lanes((SLABS, F, 128)) < 64
    chunks = [slice(at, at + CHUNK) for at in range(0, rows, CHUNK)]

    def states(g):
        left = right = jnp.zeros((ROWS, 128), F32)
        for c, at in enumerate(chunks):
            before[c, g, :, :128] = left.astype(BF16)
            before[c, g, :, 128:] = right.astype(BF16)
            state = dot(key_features(kt, dup, g, at), v_out[at, cols_of(g)])
            state = state.reshape(SLABS, PER, F, 256)
            left += jnp.where(low, state[:, 0, :, :128], state[:, 1, :, :128]).reshape(ROWS, 128)
            right += jnp.where(low, state[:, 2, :, 128:], state[:, 3, :, 128:]).reshape(ROWS, 128)
        flat[g, :, :128] = left.astype(BF16)
        flat[g, :, 128:] = right.astype(BF16)

    for g in range(GROUPS):
        if g == 2:
            late.wait()
        w = w_early[:, cols_of(g)] if g < 2 else w_late[:, cols_of(g - 2)]
        stream_tile(0, g, halo, x, w, taps, v_out, holds.at[g % 2])
        if g > 0:
            states(g - 1)
    states(GROUPS - 1)
    split = flat.reshape(n, GROUPS * ROWS // n, 256)
    for m, piece in enumerate(pieces):
        piece[...] = split[lax.rem(lax.axis_index("ctx") + m, n)]
    for copy in following:
        copy.wait()


def project_values(halo, x, w_early, streams, taps, kt, n):
    rows, width = x.shape
    half = streams.shape[2]
    part = GROUPS * ROWS // n
    return pl.pallas_call(
        values_body,
        in_specs=[VM, VM, VM, ANY, VM, VM],
        out_specs=[VM] * (4 + n),
        out_shape=[
            pltpu.VMEM((rows, half), BF16),
            pltpu.VMEM((rows // CHUNK, GROUPS, ROWS, 256), BF16),
            pltpu.VMEM(halo.shape, BF16),
            pltpu.VMEM((width, half), BF16),
        ]
        + [jax.ShapeDtypeStruct((part, 256), BF16) for _ in range(n)],
        scratch_shapes=[
            pltpu.VMEM((2, rows + 8, 256), F32),
            pltpu.VMEM((H, 2 * F, rows), F32),
            pltpu.VMEM((GROUPS, ROWS, 256), BF16),
            pltpu.VMEM((width, 512), BF16),
            pltpu.SemaphoreType.DMA((5,)),
        ],
        compiler_params=params(20),
        name="project_values",
    )(halo, x, w_early, streams, taps, kt)


def stream(number, halo, x, w, taps, out, hold):
    for j in range(w.shape[1] // 256):
        stream_tile(number, j, halo, x, w[:, cols_of(j)], taps, out, hold)


def gate_body(halo, x, w, taps, streams, out, w_next, hold, sems):
    copies = row_copies(streams.at[2], w_next, sems, 4)
    for copy in copies:
        copy.start()
    stream(1, halo, x, w, taps, out, hold)
    for copy in copies:
        copy.wait()


def project_gate(halo, x, w, taps, streams):
    rows = x.shape[0]
    return pl.pallas_call(
        gate_body,
        in_specs=[VM, VM, VM, VM, ANY],
        out_specs=[VM] * 2,
        out_shape=[pltpu.VMEM((rows, w.shape[1]), BF16), pltpu.VMEM(w.shape, BF16)],
        scratch_shapes=[pltpu.VMEM((rows + 8, 256), F32), pltpu.SemaphoreType.DMA((4,))],
        compiler_params=params(16),
        name="project_gate",
    )(halo, x, w, taps, streams)


def skip_body(halo, x, w, taps, w_o, gain, out, w_next, gain_out, hold, sems):
    copies = row_copies(w_o, w_next, sems.at[0:4], 4)
    copies.append(pltpu.make_async_copy(gain, gain_out, sems.at[4]))
    for copy in copies:
        copy.start()
    stream(2, halo, x, w, taps, out, hold)
    for copy in copies:
        copy.wait()


def project_skip(halo, x, w, taps, w_o, gain):
    rows = x.shape[0]
    return pl.pallas_call(
        skip_body,
        in_specs=[VM, VM, VM, VM, ANY, ANY],
        out_specs=[VM] * 3,
        out_shape=[
            pltpu.VMEM((rows, w.shape[1]), BF16),
            pltpu.VMEM(w_o.shape, BF16),
            pltpu.VMEM(gain.shape, F32),
        ],
        scratch_shapes=[pltpu.VMEM((rows + 8, 256), F32), pltpu.SemaphoreType.DMA((5,))],
        compiler_params=params(16),
        name="project_skip",
    )(halo, x, w, taps, w_o, gain)


def total_body(*refs):
    found = refs[0][...].astype(F32)
    for part in refs[1:-1]:
        found += part[...].astype(F32)
    refs[-1][...] = found.astype(BF16)


def add_up(parts):
    return pl.pallas_call(
        total_body,
        in_specs=[VM] * len(parts),
        out_specs=VM,
        out_shape=jax.ShapeDtypeStruct(parts[0].shape, BF16),
        compiler_params=params(8),
        name="add_up",
    )(*parts)


def starts_body(n, *refs):
    parts, earlier, outs = refs[:n], refs[n:-n], refs[-n:]
    me, block_index = lax.axis_index("ctx"), lax.axis_index("chain")
    base = jnp.zeros(parts[0].shape, F32)
    for d, block in enumerate(earlier):
        base += jnp.where(block_index > d, block[...].astype(F32), 0.0)
    known = [part[...].astype(F32) for part in parts]
    for m, out in enumerate(outs):
        peer = lax.rem(me + m, n)
        found = base
        for k, part in enumerate(known):
            found += jnp.where(lax.rem(me + n - k, n) < peer, part, 0.0)
        out[...] = found.astype(BF16)


def start_states(parts, earlier):
    n, shape = len(parts), parts[0].shape
    return pl.pallas_call(
        functools.partial(starts_body, n),
        in_specs=[VM] * (n + len(earlier)),
        out_specs=[VM] * n,
        out_shape=[jax.ShapeDtypeStruct(shape, BF16) for _ in range(n)],
        compiler_params=params(8),
        name="start_states",
    )(*parts, *earlier)


def inside_body(after, q, kt, v, out):
    half = CHUNK // 2
    lane = lanes((1, 128))
    low = lanes((half, 128)) < 64
    sides = [jnp.where((lane < 64) == side, 1.0, 0.0).astype(BF16) for side in (True, False)]
    heads = [jnp.where(lane // F == h, 1.0, 0.0).astype(BF16) for h in range(8)]
    row = lax.broadcasted_iota(jnp.int32, (128, half), 0) // F
    keep = [jnp.where(row == h, 1.0, 0.0).astype(BF16) for h in range(8)]
    first_row = lax.broadcasted_iota(jnp.int32, (half, CHUNK), 0)
    seen_first = first_row >= lanes((half, CHUNK)) % half
    seen_last = first_row + half >= lanes((half, CHUNK))

    def poly(x, seen):
        return jnp.where(seen, x * (0.5 * x + 1.0) + 1.0, 0.0).astype(BF16)

    def chunk(c, carry):
        top, bottom = pl.ds(pl.multiple_of(c * CHUNK, half), half), pl.ds(
            pl.multiple_of(c * CHUNK + half, half), half
        )
        rows = tile(c, CHUNK)
        first, last = [], []
        for part in range(2):
            keys = kt[part * 128 : (part + 1) * 128, rows]
            scaled = q[rows, part * 128 : (part + 1) * 128] * jnp.asarray(0.25, BF16)
            last.append(dot(jnp.concatenate([scaled[half:] * h for h in heads], axis=0), keys))
            for pair in range(4):
                two = [keys[:, :half] * keep[h] for h in (2 * pair, 2 * pair + 1)]
                first.append(dot(scaled[:half], jnp.concatenate(two, axis=1)))

        def weights(p):
            at = p % 4 * 2 * half
            tail = last[p // 4]
            return (
                poly(first[p], seen_first),
                poly(tail[at : at + half], seen_last),
                poly(tail[at + half : at + 2 * half], seen_last),
            )

        ready = weights(0)
        for p in range(H // 2):
            now, ready = ready, weights(p + 1) if p + 1 < H // 2 else None
            at = slice(p * 128, (p + 1) * 128)
            early = v[top, at]
            out[top, at] = dot(now[0], jnp.concatenate([early * side for side in sides], axis=0))
            whole = v[rows, at]
            out[bottom, at] = jnp.where(low, dot(now[1], whole), dot(now[2], whole))
        return carry

    lax.fori_loop(0, q.shape[0] // CHUNK, chunk, 0)


def inside(after, q, kt, v):
    return pl.pallas_call(
        inside_body,
        in_specs=[ANY, VM, VM, VM],
        out_specs=VM,
        out_shape=pltpu.VMEM(v.shape, F32),
        compiler_params=params(16),
        name="inside",
    )(after, q, kt, v)


def selection(parity):
    shape = (128, WIDE + 128)
    src = lax.broadcasted_iota(jnp.int32, shape, 0)
    col = lanes(shape)
    slab, h, i = col // 64, (col // F) % PER, col % F
    turn_by = jnp.where(slab < 9, slab, 0)
    want = parity * 64 + h * F + (i + turn_by) % F
    scale = jnp.where(slab == 0, 1.0 / 32, jnp.where(slab < 9, 1.0 / 16, 0.25))
    scale = jnp.where(slab > 9, 1.0, scale)
    scale = jnp.where((slab == 8) & (i >= 8), 0.0, scale)
    return jnp.where(src == want, scale, 0.0).astype(BF16)


def mix(start, base, chunks, q, att, before, gate, skip, gain, choose, w_o, mixed, out):
    lane = lanes((CHUNK, 128))
    one = jnp.where((lane < 64) & (lane % F == 8), 1.0, 0.0)
    wide = lanes((1, 256)) // 64
    masks = [jnp.where(wide == h, 1.0, 0.0).astype(BF16) for h in range(PER)]
    mean = lax.broadcasted_iota(jnp.int32, (256, 256), 0) // 64 == lanes((256, 256)) // 64
    mean = jnp.where(mean, 1.0 / 64, 0.0).astype(BF16)
    units = [(c, g) for c in range(chunks) for g in range(GROUPS)]
    factors, whole, mean_sq = {}, {}, {}

    def expand(u):
        c, g = units[u]
        query = q[tile(base + c), g // 2 * 128 : g // 2 * 128 + 128]
        factors[u] = dot(query, choose[g % 2])

    def carried(u):
        c, g = units[u]
        b = factors.pop(u)
        a = b[:, WIDE:]
        feats = [(a * b[:, s * 128 : (s + 1) * 128]).astype(BF16) for s in range(4)]
        b4 = b[:, 512:640]
        feats.append((jnp.where(lane < 64, a * b4, b4) + one).astype(BF16))
        state = (start[g].astype(F32) + before[base + c, g].astype(F32)).astype(BF16)
        state = state.reshape(SLABS, F, 256)
        state = jnp.stack([state * mask for mask in masks], axis=1).reshape(WIDE, 256)
        whole[u] = att[tile(base + c), cols_of(g)] + dot(jnp.concatenate(feats, axis=1), state)

    def squares(u):
        mean_sq[u] = dot((whole[u] * whole[u]).astype(BF16), mean)

    def gated(u):
        c, g = units[u]
        rows, at = tile(base + c), cols_of(g)
        normed = (whole.pop(u) * lax.rsqrt(mean_sq.pop(u) + EPS)).astype(BF16).astype(F32)
        gates = gate[rows, at].astype(F32)
        act = 0.5 * gates * (1.0 + jnp.tanh(0.5 * gates))
        made = act * (normed * gain[:, at] + skip[rows, at].astype(F32))
        mixed[c * CHUNK : (c + 1) * CHUNK, at] = made.astype(BF16)

    def product(u):
        c, j = units[u]
        rows, at = slice(c * CHUNK, (c + 1) * CHUNK), slice(j * 512, (j + 1) * 512)
        out[rows, at] = dot(mixed[rows], w_o[:, at]).astype(BF16)

    stages = ((expand, 0), (carried, 1), (squares, 2), (gated, 3), (product, 3 + GROUPS))
    for t in range(len(units) + 3 + GROUPS):
        for stage, lag in stages:
            if 0 <= t - lag < len(units):
                stage(t - lag)


def gather_start(pieces, start):
    n = len(pieces)
    split = start.reshape(n, GROUPS * ROWS // n, 256)
    for m, piece in enumerate(pieces):
        split[lax.rem(lax.axis_index("ctx") + n - m, n)] = piece[...]


def finish_body(away, after, q, att, before, gate, skip, gain, choose, w_o, *rest):
    pieces, (out, start, mixed) = rest[:-3], rest[-3:]
    gather_start(pieces, start)
    chunks = out.shape[0] // CHUNK
    core = lax.axis_index("tp")
    base = chunks * (1 - core if away else core)
    mix(start, base, chunks, q, att, before, gate, skip, gain, choose, w_o, mixed, out)


def finish(away, after, tail, w_o, pieces, rows):
    half, width = w_o.shape
    return pl.pallas_call(
        functools.partial(finish_body, away),
        in_specs=[ANY] + [VM] * (len(tail) + 1 + len(pieces)),
        out_specs=VM,
        out_shape=pltpu.VMEM((rows, width), BF16),
        scratch_shapes=[pltpu.VMEM((GROUPS, ROWS, 256), BF16), pltpu.VMEM((rows, half), BF16)],
        compiler_params=params(16),
        name="away" if away else "home",
    )(after, *tail, w_o, *pieces)


def join_body(own, other, out, hold, sems):
    copies = []
    size = out.shape[0] // 8
    for i in range(8):
        at = slice(i * size, (i + 1) * size)
        hold[at] = (own[at].astype(F32) + other[at].astype(F32)).astype(BF16)
        copies.append(pltpu.make_async_copy(hold.at[at], out.at[at], sems.at[i]))
        copies[-1].start()
    for copy in copies:
        copy.wait()


def join(own, other):
    return pl.pallas_call(
        join_body,
        in_specs=[VM, VM],
        out_specs=pl.BlockSpec(memory_space=pltpu.HBM),
        out_shape=jax.ShapeDtypeStruct(other.shape, BF16),
        scratch_shapes=[pltpu.VMEM(other.shape, BF16), pltpu.SemaphoreType.DMA((8,))],
        compiler_params=params(8),
        name="join",
    )(own, other)


def shift(block, axes, distance, size):
    return lax.ppermute(block, axes, [(i, i + distance) for i in range(size - distance)])


def turn(block, axis, distance, size):
    return lax.ppermute(block, axis, [(i, (i + distance) % size) for i in range(size)])


def per_device(tokens, w_in, conv_w, w_q, w_k, gain, w_o):
    rows, width = tokens.shape
    half = w_in.shape[3]
    n, blocks = lax.axis_size("ctx"), lax.axis_size("chain")
    streams = in_hbm(w_in.transpose(1, 2, 0, 3).reshape(3, width, half))
    w_out = in_hbm(w_o.reshape(half, width))

    halo = shift(tokens[rows - 8 :], ("chain", "ctx"), 1, n * blocks)
    q, kt, x, taps, w_early, choose = project_qk(tokens, w_q, w_k, conv_w, streams)
    values, before, halo, w_gate, *mine = project_values(
        halo, x, w_early, streams, taps, kt, n
    )
    theirs = [mine[0]] + [turn(mine[m], "ctx", m, n) for m in range(1, n)]
    gate, w_skip = project_gate(halo, x, w_gate, taps, streams)
    theirs, gate = lax.optimization_barrier((theirs, gate))
    total = add_up(theirs)
    earlier = [turn(total, "chain", d, blocks) for d in range(1, blocks)]
    skip, weight, gains = project_skip(halo, x, w_skip, taps, w_out, in_hbm(gain))
    earlier, skip = lax.optimization_barrier((earlier, skip))
    starts = start_states(theirs, earlier)
    got = [starts[0]] + [turn(starts[m], "ctx", m, n) for m in range(1, n)]
    att = inside(starts[0], q, kt, values)
    got, att = lax.optimization_barrier((got, att))
    tail = (q, att, before, gate, skip, gains, choose)
    sent = finish(True, att, tail, weight, got, rows // 2)
    swapped = lax.ppermute(sent, "tp", [(0, 1), (1, 0)])
    kept = finish(False, sent, tail, weight, got, rows // 2)
    return join(kept, swapped)


def solution(mesh):
    return jax.shard_map(
        per_device,
        mesh=mesh,
        in_specs=(
            P(("chain", "ctx"), None),
            P(None, None, "tp", None),
            P(None, None, "tp", None),
            P(),
            P(),
            P("tp", None),
            P("tp", None, None),
        ),
        out_specs=P(("chain", "ctx", "tp"), None),
        check_vma=False,
    )
```
